32 devices in a mesh: grp: 2 (over y), seq: 4 (over z), req: 2 (over x), hd: 2 (over core).
Axes of the slice: x: 2, y: 2, z: 4, core: 2. Of those that a mesh axis runs over, the one named last changes fastest.
Arguments:
- cache: bfloat16 [8, 8, 1536, 256], P(('grp', 'req'), 'hd', 'seq'), parts along dimension 0, may hold values from -7 to 7
- evicted: bfloat16 [8, 8, 256, 256], P(('grp', 'req'), 'hd', 'seq'), parts along dimension 0, may hold values from -6 to 6
- merge_weight: bfloat16 [8, 8, 256], P(('grp', 'req'), 'hd', 'seq'), parts along dimension 0, may hold values from 0.25 to 2.5
- targets: int32 [8, 8, 256], P(('grp', 'req'), 'hd', 'seq'), parts along dimension 0, may hold values from 0 to 1535, as said below
- kept_counts: int32 [8, 4], P(('grp', 'req'), 'seq'), parts along dimension 0, may hold values from 192 to 384, as said below
- queries: bfloat16 [4, 8, 64, 128], P(None, ('grp', 'req'), 'hd'), parts along dimension 1, may hold values from -1024 to 1024
- new_rows: bfloat16 [4, 8, 8, 256], P(None, ('grp', 'req'), 'hd'), parts along dimension 1, may hold values from -8 to 8
Outputs:
- merged_cache: bfloat16 [8, 8, 1536, 256], P(('grp', 'req'), 'hd', 'seq'), parts along dimension 0
- attended: bfloat16 [4, 8, 64, 128], P(None, ('grp', 'req'), 'hd'), parts along dimension 1
The draws below stay inside these ranges and needn't reach their ends.
There are 2 independent parts, one for each index of `grp`. The reference program is written for one: setup_inputs(seed, part) draws one part's arguments, and reference() takes and returns one part's arrays. A program takes and returns all parts, laid end to end along the dimension named above; each array names one. Nothing has to cross between parts.
Inputs may be any that keep to these rules, and one draw needn't show every extreme that they name: `targets`: for each request, head and block of 64 evicted rows, at most 32 rows target one block of 384 kept positions; every target is a live position. `kept_counts`: each request has a block with all 384 positions live.
All inputs are finite; a program needn't handle non-finite values.
Results may differ from the reference program's by a relative error of at most 0.0029.
Values may be sent and summed in bfloat16 or wider, within the bound.
A program may use at most 64 MiB of HBM per device.

```python
import math
import jax
import jax.numpy as jnp
from jax import lax

KVH = 8
QH = 64
HEAD = 128
KEPT_DEV = 384
EVICT_DEV = 64
STEPS = 4
REQS = 4
KEPT = 1536
EVICT = 256


def routing_tables(key):
    shards = KEPT // KEPT_DEV
    counts = jax.random.randint(jax.random.fold_in(key, 11), (REQS, shards), KEPT_DEV // 2, KEPT_DEV + 1)
    full_at = jax.random.randint(jax.random.fold_in(key, 12), (REQS,), 0, shards)
    counts = jnp.where(jnp.arange(shards)[None, :] == full_at[:, None], KEPT_DEV, counts)
    capacity = max(2, 2 * EVICT_DEV // shards)
    hottest = jax.random.randint(jax.random.fold_in(key, 13), (REQS, KVH), 0, shards)
    others_total = (shards - 1) * capacity
    spare = EVICT_DEV - capacity
    noise = jax.random.randint(jax.random.fold_in(key, 14), (REQS, KVH, shards, others_total), 0, 1 << 16)
    noise = noise * 4096 + jnp.arange(others_total)
    chosen = jnp.argsort(noise, axis=-1, stable=True)[..., :spare]
    other_dest = chosen // capacity
    other_dest = other_dest + (other_dest >= hottest[:, :, None, None]).astype(jnp.int32)
    hot_dest = jnp.broadcast_to(hottest[:, :, None, None], (REQS, KVH, shards, capacity))
    destination = jnp.concatenate([hot_dest, other_dest], axis=-1)
    shuffle = jax.random.randint(jax.random.fold_in(key, 15), (REQS, KVH, shards, EVICT_DEV), 0, 1 << 16)
    shuffle = shuffle * 4096 + jnp.arange(EVICT_DEV)
    ordering = jnp.argsort(shuffle, axis=-1, stable=True)
    destination = jnp.take_along_axis(destination, ordering, axis=-1)
    count_table = jnp.broadcast_to(counts[:, None, None, :], (REQS, KVH, shards, shards))
    limit = jnp.take_along_axis(count_table, destination, axis=-1)
    position = jax.random.randint(jax.random.fold_in(key, 16), destination.shape, 0, limit)
    aimed = destination * KEPT_DEV + position
    return (counts.astype(jnp.int32), aimed.reshape(REQS, KVH, shards * EVICT_DEV).astype(jnp.int32))


def draw_targets(key, part):
    return routing_tables(key)[1]


def draw_kept_counts(key, part):
    return routing_tables(key)[0]


def draw_cache(key, part):
    shards = KEPT // KEPT_DEV
    key_part = jnp.clip(jax.random.normal(jax.random.fold_in(key, 31), (REQS, KVH, KEPT, HEAD)), -5.0, 5.0)
    offsets = jax.random.uniform(jax.random.fold_in(key, 32), (REQS, KVH, shards, 1, HEAD), minval=-1.5, maxval=1.5)
    value_base = jnp.clip(jax.random.normal(jax.random.fold_in(key, 33), (REQS, KVH, shards, KEPT_DEV, HEAD)), -4.0, 4.0)
    value_part = (value_base + offsets).reshape(REQS, KVH, KEPT, HEAD)
    return jnp.concatenate([key_part, value_part], axis=-1).astype(jnp.bfloat16)


def decode_inputs(key):
    query_key = jax.random.fold_in(key, 21)
    fresh_key = jax.random.fold_in(key, 22)
    asked = jnp.clip(jax.random.normal(query_key, (STEPS, REQS, QH, HEAD)), -6.0, 6.0)
    fresh = jnp.clip(jax.random.normal(fresh_key, (STEPS, REQS, KVH, 2 * HEAD)), -6.0, 6.0)
    return (asked, fresh)


def draw_queries(key, part):
    return decode_inputs(key)[0].astype(jnp.bfloat16)


def draw_new_rows(key, part):
    return decode_inputs(key)[1].astype(jnp.bfloat16)


def shard_levels(rng, extent, pieces, smallest, largest):
    def one(dim, parts):
        heights = jax.random.uniform(jax.random.fold_in(jax.random.fold_in(rng, 6), dim), (parts,), jnp.float32, smallest / len(pieces), largest / len(pieces))
        return jnp.repeat(jnp.exp(heights), extent[dim] // parts).reshape((-1,) + (1,) * (len(extent) - dim - 1))

    gain = one(*pieces[0])
    for cut in pieces[1:]:
        gain = gain * one(*cut)
    return gain


def centred(rng, dims, spread, bound, pieces=(), kind=jnp.bfloat16):
    array = jax.random.normal(rng, dims, jnp.float32) * spread
    if len(pieces) > 0:
        array = shard_levels(rng, dims, pieces, -0.22, 0.18) * array
    return jnp.clip(array, min=-bound, max=bound).astype(kind)


def setup_inputs(seed: int = 0, part: int = 0) -> dict:
    splits = jax.random.split(jax.random.key(seed), 8)
    own_keys = jax.random.split(jax.random.fold_in(splits[7], part), 8)
    return {
        "cache": draw_cache(jax.random.fold_in(jax.random.fold_in(splits[7], part), 71), part),
        "evicted": centred(own_keys[1], (REQS, KVH, EVICT, 2 * HEAD), 1.0, 6.0, ((0, 2), (1, 2), (2, 4))),
        "merge_weight": jnp.clip(jnp.exp(math.log(2.5) - 2.3025851 * jax.random.uniform(own_keys[2], (REQS, KVH, EVICT), jnp.float32) ** shard_levels(own_keys[2], (REQS, KVH, EVICT), ((0, 2), (1, 2), (2, 4)), -0.2, 0.2)), 0.25, 2.5).astype(jnp.bfloat16),
        "targets": draw_targets(jax.random.fold_in(jax.random.fold_in(splits[7], part), 71), part),
        "kept_counts": draw_kept_counts(jax.random.fold_in(jax.random.fold_in(splits[7], part), 71), part),
        "queries": draw_queries(jax.random.fold_in(jax.random.fold_in(splits[7], part), 71), part),
        "new_rows": draw_new_rows(jax.random.fold_in(jax.random.fold_in(splits[7], part), 71), part),
    }


def merge_head(inputs):
    stored, removed, weights, target_rows = inputs
    weight_f = weights.astype(jnp.float32)
    summed = jax.ops.segment_sum(weight_f[:, None] * removed.astype(jnp.float32), target_rows, num_segments=KEPT)
    weight_sum = jax.ops.segment_sum(weight_f, target_rows, num_segments=KEPT)
    return ((stored.astype(jnp.float32) + summed) / (1.0 + weight_sum)[:, None]).astype(jnp.bfloat16)

def round_weights(values):
    rounded = values.astype(jnp.bfloat16)
    rounded = lax.optimization_barrier(rounded)
    return rounded.astype(jnp.float32)

def attend_request(inputs):
    stored, counts, asked_rows, fresh_rows = inputs
    group_size = QH // KVH
    blocks_count = KEPT // KEPT_DEV
    scale_factor = 1.0 / math.sqrt(HEAD)
    query_rows = asked_rows.reshape(STEPS, KVH, group_size, HEAD).transpose(1, 0, 2, 3)
    query_rows = query_rows.reshape(KVH, STEPS * group_size, HEAD).astype(jnp.float32)
    key_blocks = stored[:, :, :HEAD].astype(jnp.float32).reshape(KVH, blocks_count, KEPT_DEV, HEAD)
    value_blocks = stored[:, :, HEAD:].astype(jnp.float32).reshape(KVH, blocks_count, KEPT_DEV, HEAD)
    scores = jnp.einsum('hqd,hbkd->hbqk', query_rows, key_blocks) * scale_factor
    living = jnp.arange(KEPT_DEV, dtype=jnp.int32)[None, :] < counts[:, None]
    scores = jnp.where(living[None, :, None, :], scores, -1e+30)
    block_max = lax.optimization_barrier(jnp.max(scores, axis=-1))
    exponent = jnp.exp(scores - block_max[..., None])
    block_sum = lax.optimization_barrier(jnp.sum(exponent, axis=-1))
    block_acc = jnp.einsum('hbqk,hbkd->hbqd', round_weights(exponent), value_blocks)
    fresh_heads = fresh_rows.transpose(1, 0, 2).astype(jnp.float32)
    new_scores = jnp.einsum('hqd,hjd->hqj', query_rows, fresh_heads[:, :, :HEAD]) * scale_factor
    step_index = jnp.arange(STEPS * group_size, dtype=jnp.int32) // group_size
    allowed = jnp.arange(STEPS, dtype=jnp.int32)[None, :] <= step_index[:, None]
    new_scores = jnp.where(allowed[None], new_scores, -1e+30)
    new_max = lax.optimization_barrier(jnp.max(new_scores, axis=-1))
    new_exponent = jnp.exp(new_scores - new_max[..., None])
    new_sum = lax.optimization_barrier(jnp.sum(new_exponent, axis=-1))
    new_acc = jnp.einsum('hqj,hjd->hqd', round_weights(new_exponent), fresh_heads[:, :, HEAD:])
    highest = jnp.maximum(lax.optimization_barrier(jnp.max(block_max, axis=1)), new_max)
    block_scale = jnp.exp(block_max - highest[:, None, :])
    new_scale = jnp.exp(new_max - highest)
    denominator = lax.optimization_barrier(jnp.sum(block_sum * block_scale, axis=1)) + new_sum * new_scale
    numerator = lax.optimization_barrier(jnp.sum(block_acc * block_scale[..., None], axis=1)) + new_acc * new_scale[..., None]
    result = (numerator / denominator[..., None]).astype(jnp.bfloat16)
    result = result.reshape(KVH, STEPS, group_size, HEAD).transpose(1, 0, 2, 3)
    return result.reshape(STEPS, QH, HEAD)

def reference(cache, evicted, merge_weight, targets, kept_counts, queries, new_rows):
    merged_flat = lax.map(merge_head, (cache.reshape(REQS * KVH, KEPT, 2 * HEAD), evicted.reshape(REQS * KVH, EVICT, 2 * HEAD), merge_weight.reshape(REQS * KVH, EVICT), targets.reshape(REQS * KVH, EVICT)))
    merged_cache = merged_flat.reshape(REQS, KVH, KEPT, 2 * HEAD)
    attended = lax.map(attend_request, (merged_cache, kept_counts, queries.transpose(1, 0, 2, 3), new_rows.transpose(1, 0, 2, 3)))
    return (merged_cache, attended.transpose(1, 0, 2, 3))
```

```python
import functools
import math

import jax
import jax.numpy as jnp
from jax import lax
from jax.experimental import pallas as pl
from jax.experimental.pallas import tpu as pltpu
from jax.sharding import PartitionSpec as P

F32 = jnp.float32
BF16 = jnp.bfloat16
NEG = -1e30


def contract_last(a, b):
    return lax.dot_general(a, b, (((1,), (1,)), ((), ())), preferred_element_type=F32)


def softmax_block(query, keys, values, allowed, scale):
    scores = jnp.where(allowed, contract_last(query, keys) * scale, NEG)
    highest = jnp.max(scores, axis=-1, keepdims=True)
    exponent = jnp.exp(scores - highest)
    total = jnp.sum(exponent, axis=-1, keepdims=True)
    weighted = jnp.dot(exponent.astype(BF16), values, preferred_element_type=F32)
    return highest, total, weighted


def kernel(
    shards, cap, groups, plan,
    cache, evicted, weight, target, counts, queries, fresh,
    merged, attended,
    evict_v, weight_v, target_v, counts_v, query_v, fresh_v,
    send, recv, meta_send, meta_recv, query_s, fresh_o, fresh_ml,
    part, part_m, part_recv, part_m_recv, shared, shared_m, result,
    in_sem, cache_sem, row_ssem, row_rsem, meta_ssem, meta_rsem,
    part_ssem, part_rsem, share_ssem, share_rsem, res_ssem, res_rsem,
):
    reqs, heads, kept, width = merged.shape
    pairs = reqs * heads
    evict = evict_v.shape[2]
    steps, _, _, depth = query_v.shape
    rows = query_s.shape[1]
    group = rows // steps
    slots = shards * cap
    scale = 1.0 / math.sqrt(depth)
    me = lax.axis_index("seq")
    core = lax.axis_index("hd")

    def peer(d):
        return lax.rem(me + d, shards)

    def source(d):
        return lax.rem(me + shards - d, shards)

    def remote(src, dst, ssem, rsem, device):
        return pltpu.make_async_remote_copy(
            src_ref=src, dst_ref=dst, send_sem=ssem, recv_sem=rsem,
            device_id={"seq": device}, device_id_type=pl.DeviceIdType.MESH,
        )

    small = [
        pltpu.make_async_copy(src, dst, in_sem.at[i])
        for i, (src, dst) in enumerate((
            (target, target_v), (weight, weight_v), (evicted, evict_v),
            (queries, query_v), (fresh, fresh_v), (counts, counts_v),
        ))
    ]
    for copy in small:
        copy.start()
    loads = []
    for i in range(pairs):
        r, h = divmod(i, heads)
        loads.append(pltpu.make_async_copy(cache.at[r, h], merged.at[r, h], cache_sem.at[i]))
        loads[i].start()

    barrier = pltpu.get_barrier_semaphore()
    for d in range(1, shards):
        pl.semaphore_signal(
            barrier, inc=1, device_id={"seq": peer(d)}, device_id_type=pl.DeviceIdType.MESH
        )

    diagonal = lax.broadcasted_iota(jnp.int32, (rows, 128), 0) == lax.broadcasted_iota(
        jnp.int32, (rows, 128), 1
    )

    def to_rows(*columns):
        flat = [jnp.sum(jnp.where(diagonal, c, 0.0), axis=0, keepdims=True) for c in columns]
        return jnp.concatenate(flat, axis=0)

    def to_column(row):
        return jnp.sum(jnp.where(diagonal, row, 0.0), axis=1, keepdims=True)

    def attend_new():
        padded = -(-steps // 16) * 16
        new_step = lax.broadcasted_iota(jnp.int32, (rows, padded), 1)
        row_index = lax.broadcasted_iota(jnp.int32, (rows, padded), 0)
        allowed = row_index < 0
        for s in range(steps):
            allowed = allowed | ((new_step == s) & (row_index >= s * group))
        for r in range(reqs):
            asked = [query_v[s, r].astype(F32) for s in range(steps)]
            added = [fresh_v[s, r].astype(F32) for s in range(steps)]
            for h in range(heads):
                i = r * heads + h
                query = jnp.concatenate(
                    [a[h * group : (h + 1) * group] for a in asked], axis=0
                ).astype(BF16)
                query_s[i] = query
                latest = jnp.concatenate(
                    [a[h : h + 1] for a in added] + [jnp.zeros((padded - steps, width), F32)],
                    axis=0,
                ).astype(BF16)
                highest, total, weighted = softmax_block(
                    query, latest[:, :depth], latest[:, depth:], allowed, scale
                )
                fresh_o[i] = weighted
                fresh_ml[i, 0:2, :] = to_rows(highest, total)

    for copy in small[3:]:
        copy.wait()

    @pl.when(core != 0)
    def _():
        attend_new()

    for copy in small[:3]:
        copy.wait()
    aimed = jnp.concatenate([target_v[r] for r in range(reqs)], axis=0)
    weights = jnp.concatenate([weight_v[r].astype(F32) for r in range(reqs)], axis=0)
    owned, position, base = [], jnp.zeros_like(aimed), jnp.zeros(aimed.shape, F32)
    for d in range(shards):
        low = peer(d) * kept
        mine = (aimed >= low) & (aimed < low + kept)
        owned.append(jnp.where(mine, 1.0, 0.0))
        position = jnp.where(mine, aimed - low, position)
        base = jnp.where(mine, float(d * cap), base)
    above = lax.broadcasted_iota(jnp.int32, (evict, evict), 0) < lax.broadcasted_iota(
        jnp.int32, (evict, evict), 1
    )
    earlier = jnp.dot(
        jnp.concatenate(owned, axis=0).astype(BF16),
        jnp.where(above, 1.0, 0.0).astype(BF16),
        preferred_element_type=F32,
    )
    slot = base
    for d in range(shards):
        slot = slot + owned[d] * earlier[d * pairs : (d + 1) * pairs]
    slot = slot.astype(jnp.int32)
    features = jnp.concatenate(
        [weights, (position & 255).astype(F32), (position >> 8).astype(F32)], axis=0
    ).astype(BF16)
    slot_row = lax.broadcasted_iota(jnp.int32, (slots, evict), 0)
    for i in range(pairs):
        r, h = divmod(i, heads)
        packing = jnp.where(slot_row == slot[i : i + 1, :], 1.0, 0.0).astype(BF16)
        packed = jnp.dot(packing, evict_v[r, h], preferred_element_type=F32).astype(BF16)
        send[i] = packed
        recv[i, 0:cap, :] = packed[0:cap]
        meta = contract_last(features, packing)
        meta_send[i : i + 1, :] = (
            (meta[2 * pairs + i : 2 * pairs + i + 1] * 256.0 + meta[pairs + i : pairs + i + 1])
            * 2048.0 + meta[i : i + 1] * 512.0
        )

    pl.semaphore_wait(barrier, shards - 1)

    meta_copies = {}
    for d in range(1, shards):
        meta_copies[d] = remote(
            meta_send, meta_recv.at[d], meta_ssem.at[d], meta_rsem.at[d], peer(d)
        )
        meta_copies[d].start()
    span = pairs // groups
    row_copies = {}
    for g in range(groups):
        for d in range(1, shards):
            lot = (pl.ds(g * span, span), pl.ds(d * cap, cap))
            row_copies[g, d] = remote(
                send.at[lot], recv.at[lot], row_ssem.at[g, d], row_rsem.at[g, d], peer(d)
            )
            row_copies[g, d].start()

    @pl.when(core == 0)
    def _():
        attend_new()

    for d in range(1, shards):
        meta_copies[d].wait_recv()
    lane = lax.broadcasted_iota(jnp.int32, (pairs, slots), 1)
    meta = meta_send[...]
    for d in range(1, shards):
        meta = jnp.where(lane >= d * cap, meta_recv[d], meta)
    slot_position = (meta * (1.0 / 2048.0)).astype(jnp.int32)
    slot_weight = (meta - slot_position.astype(F32) * 2048.0) * (1.0 / 512.0)

    kept_row = lax.broadcasted_iota(jnp.int32, (kept, slots), 0)
    kept_lane = lax.broadcasted_iota(jnp.int32, (rows, kept), 1)
    ones = jnp.ones((slots, 128), BF16)

    def merge(i):
        r, h = divmod(i, heads)
        loads[i].wait()
        if groups == pairs:
            for d in range(1, shards):
                row_copies[i, d].wait_recv()
        elif i == 0:
            for copy in row_copies.values():
                copy.wait_recv()
        placing = jnp.where(
            kept_row == slot_position[i : i + 1], slot_weight[i : i + 1], 0.0
        ).astype(BF16)
        summed = jnp.dot(placing, recv[i], preferred_element_type=F32)
        factor = 1.0 / (1.0 + jnp.dot(placing, ones, preferred_element_type=F32))
        factor = jnp.concatenate([factor] * (width // 128), axis=1)
        fused = ((merged[r, h].astype(F32) + summed) * factor).astype(BF16)
        merged[r, h] = fused
        return softmax_block(
            query_s[i], fused[:, :depth], fused[:, depth:], kept_lane < counts_v[:, r : r + 1], scale
        )

    def part_pair(k, count, away, device):
        lot = pl.ds(0, count * rows)
        return (
            remote(
                part.at[k, lot], part_recv.at[k, away, lot],
                part_ssem.at[k, 0], part_rsem.at[k, away, 0], device,
            ),
            remote(
                part_m.at[k], part_m_recv.at[k, away],
                part_ssem.at[k, 1], part_rsem.at[k, away, 1], device,
            ),
        )

    def share_pair(k, count, origin, d):
        lot = shared.at[k, origin, pl.ds(0, count * rows)]
        top = shared_m.at[k, origin]
        return (
            remote(lot, lot, share_ssem.at[k, d, 0], share_rsem.at[k, d, 0], peer(d)),
            remote(top, top, share_ssem.at[k, d, 1], share_rsem.at[k, d, 1], peer(d)),
        )

    def to_owner(k, count, owner):
        return part_pair(k, count, lax.rem(owner - me + shards, shards), owner)

    def send_result(k, first, count, d):
        lot = result.at[pl.ds(first, count)]
        return remote(lot, lot, res_ssem.at[k, d], res_rsem.at[k], peer(d))

    owned_plan = [(k, *entry) for k, entry in enumerate(plan) if entry[2] is not None]
    owned_index = {entry[0]: n for n, entry in enumerate(owned_plan)}
    shared_plan = [(k, *entry) for k, entry in enumerate(plan) if entry[2] is None]
    shared_index = {entry[0]: n for n, entry in enumerate(shared_plan)}

    for k, (first, count, owner) in enumerate(plan):
        for j in range(count):
            highest, total, weighted = merge(first + j)
            size = jnp.maximum(jnp.max(jnp.abs(weighted), axis=-1, keepdims=True), 1e-30)
            coded = jnp.round(weighted * (32767.0 / size)).astype(jnp.int32).astype(jnp.int16)
            if owner is None:
                into, into_m = shared.at[shared_index[k], me], shared_m.at[shared_index[k], me]
            else:
                into, into_m = part.at[owned_index[k]], part_m.at[owned_index[k]]
            into[j * rows : (j + 1) * rows, :] = coded
            into_m[3 * j : 3 * j + 3, :] = to_rows(highest, total, size * (1.0 / 32767.0))
        if owner is None:
            for d in range(1, shards):
                for copy in share_pair(shared_index[k], count, me, d):
                    copy.start()
        else:
            @pl.when(me != owner)
            def _():
                for copy in to_owner(owned_index[k], count, owner):
                    copy.start()

    lanes = lax.broadcasted_iota(jnp.int32, (1, 128), 1)

    def combine(first, count, blocks):
        for j in range(count):
            i = first + j
            tiles = [fresh_ml[i, 0:2, :]] + [m[3 * j : 3 * j + 3, :] for _, m in blocks]
            outs = [fresh_o[i]] + [
                b[j * rows : (j + 1) * rows, :].astype(jnp.int32).astype(F32) for b, _ in blocks
            ]
            top = tiles[0][0:1]
            for tile in tiles[1:]:
                top = jnp.maximum(top, tile[0:1])
            shares = [jnp.exp(tile[0:1] - top) for tile in tiles]
            total = shares[0] * tiles[0][1:2]
            for share, tile in zip(shares[1:], tiles[1:]):
                total = total + share * tile[1:2]
            total = jnp.where(lanes < rows, total, 1.0)
            blend = to_column(shares[0] / total) * outs[0]
            for share, tile, out in zip(shares[1:], tiles[1:], outs[1:]):
                blend = blend + to_column(share * tile[2:3] / total) * out
            result[i] = blend.astype(BF16)

    for k, first, count, owner in owned_plan:
        n = owned_index[k]

        @pl.when(me == owner)
        def _():
            for d in range(1, shards):
                for copy in part_pair(n, count, d, peer(d)):
                    copy.wait_recv()
            combine(
                first, count,
                [(part.at[n], part_m.at[n])]
                + [(part_recv.at[n, d], part_m_recv.at[n, d]) for d in range(1, shards)],
            )
            for d in range(1, shards):
                send_result(n, first, count, d).start()

    for k, first, count, _ in shared_plan:
        n = shared_index[k]
        for d in range(1, shards):
            for copy in share_pair(n, count, source(d), d):
                copy.wait_recv()
        combine(first, count, [(shared.at[n, d], shared_m.at[n, d]) for d in range(shards)])

    for k, first, count, owner in owned_plan:
        @pl.when(me != owner)
        def _():
            send_result(owned_index[k], first, count, 1).wait_recv()

    for r in range(reqs):
        done = [result[r * heads + h].astype(F32) for h in range(heads)]
        for s in range(steps):
            attended[s, r] = jnp.concatenate(
                [a[s * group : (s + 1) * group] for a in done], axis=0
            ).astype(BF16)

    for copy in list(meta_copies.values()) + list(row_copies.values()):
        copy.wait_send()
    for k, first, count, owner in owned_plan:
        n = owned_index[k]

        @pl.when(me != owner)
        def _():
            for copy in to_owner(n, count, owner):
                copy.wait_send()

        @pl.when(me == owner)
        def _():
            for d in range(1, shards):
                send_result(n, first, count, d).wait_send()

    for k, first, count, _ in shared_plan:
        for d in range(1, shards):
            for copy in share_pair(shared_index[k], count, me, d):
                copy.wait_send()


def write_out(merged, attended, merged_out, attended_out, sem):
    copies = [
        pltpu.make_async_copy(merged, merged_out, sem.at[0]),
        pltpu.make_async_copy(attended, attended_out, sem.at[1]),
    ]
    for copy in copies:
        copy.start()
    for copy in copies:
        copy.wait()


def schedule(shards, pairs):
    per = max(1, pairs // shards)
    firsts = list(range(0, pairs, per))
    late = len(firsts) // 2 if shards <= 8 else 0
    return tuple(
        (first, min(per, pairs - first), None)
        if n >= len(firsts) - late
        else (first, min(per, pairs - first), (shards // 2 - 1 + n) % shards)
        for n, first in enumerate(firsts)
    )


def body(shards, cache, evicted, merge_weight, targets, kept_counts, queries, new_rows):
    reqs, heads, kept, width = cache.shape
    pairs = reqs * heads
    evict = evicted.shape[2]
    steps, _, query_local, depth = queries.shape
    rows = steps * query_local // heads
    cap = -(-max(2, 2 * evict // shards) // 16) * 16
    slots = shards * cap
    groups = pairs if shards <= 8 else 1
    plan = schedule(shards, pairs)
    most = max(count for _, count, _ in plan)
    owned = max(1, sum(owner is not None for _, _, owner in plan))
    common = max(1, len(plan) - owned)
    high = -(-3 * most // 8) * 8
    dma = pltpu.SemaphoreType.DMA
    done = pl.pallas_call(
        functools.partial(kernel, shards, cap, groups, plan),
        out_shape=(
            jax.ShapeDtypeStruct(cache.shape, BF16),
            jax.ShapeDtypeStruct(queries.shape, BF16),
        ),
        in_specs=[pl.BlockSpec(memory_space=pltpu.HBM)] * 7,
        out_specs=(pl.BlockSpec(memory_space=pltpu.VMEM),) * 2,
        scratch_shapes=[
            pltpu.VMEM(evicted.shape, BF16),
            pltpu.VMEM(merge_weight.shape, BF16),
            pltpu.VMEM(targets.shape, jnp.int32),
            pltpu.VMEM(kept_counts.shape[::-1], jnp.int32),
            pltpu.VMEM(queries.shape, BF16),
            pltpu.VMEM(new_rows.shape, BF16),
            pltpu.VMEM((pairs, slots, width), BF16),
            pltpu.VMEM((pairs, slots, width), BF16),
            pltpu.VMEM((pairs, slots), F32),
            pltpu.VMEM((shards, pairs, slots), F32),
            pltpu.VMEM((pairs, rows, depth), BF16),
            pltpu.VMEM((pairs, rows, depth), F32),
            pltpu.VMEM((pairs, 8, 128), F32),
            pltpu.VMEM((owned, most * rows, depth), jnp.int16),
            pltpu.VMEM((owned, high, 128), F32),
            pltpu.VMEM((owned, shards, most * rows, depth), jnp.int16),
            pltpu.VMEM((owned, shards, high, 128), F32),
            pltpu.VMEM((common, shards, most * rows, depth), jnp.int16),
            pltpu.VMEM((common, shards, high, 128), F32),
            pltpu.VMEM((pairs, rows, depth), BF16),
            dma((6,)),
            dma((pairs,)),
            dma((groups, shards)),
            dma((groups, shards)),
            dma((shards,)),
            dma((shards,)),
            dma((owned, 2)),
            dma((owned, shards, 2)),
            dma((common, shards, 2)),
            dma((common, shards, 2)),
            dma((owned, shards)),
            dma((owned,)),
        ],
        compiler_params=pltpu.CompilerParams(
            collective_id=0, has_side_effects=True, vmem_limit_bytes=48 * 1024 * 1024
        ),
    )(*(
        pltpu.with_memory_space_constraint(a, pltpu.HBM)
        for a in (cache, evicted, merge_weight, targets, kept_counts.T, queries, new_rows)
    ))
    return pl.pallas_call(
        write_out,
        out_shape=tuple(jax.ShapeDtypeStruct(a.shape, a.dtype) for a in done),
        in_specs=[pl.BlockSpec(memory_space=pltpu.VMEM)] * 2,
        out_specs=(pl.BlockSpec(memory_space=pltpu.HBM),) * 2,
        scratch_shapes=[dma((2,))],
    )(*(pltpu.with_memory_space_constraint(a, pltpu.VMEM) for a in done))


def solution(mesh):
    return jax.shard_map(
        functools.partial(body, mesh.shape["seq"]),
        mesh=mesh,
        in_specs=(
            P(("grp", "req"), "hd", "seq", None),
            P(("grp", "req"), "hd", "seq", None),
            P(("grp", "req"), "hd", "seq"),
            P(("grp", "req"), "hd", "seq"),
            P(("grp", "req"), "seq"),
            P(None, ("grp", "req"), "hd", None),
            P(None, ("grp", "req"), "hd", None),
        ),
        out_specs=(P(("grp", "req"), "hd", "seq", None), P(None, ("grp", "req"), "hd", None)),
        check_vma=False,
    )
```

```python
import functools
import math

import jax
import jax.numpy as jnp
from jax import lax
from jax.experimental import pallas as pl
from jax.experimental.pallas import tpu as pltpu
from jax.sharding import PartitionSpec as P

F32 = jnp.float32
BF16 = jnp.bfloat16
NEG = -1e30


def contract_last(a, b):
    return lax.dot_general(a, b, (((1,), (1,)), ((), ())), preferred_element_type=F32)


def softmax_block(query, keys, values, allowed, scale):
    scores = jnp.where(allowed, contract_last(query, keys) * scale, NEG)
    highest = jnp.max(scores, axis=-1, keepdims=True)
    exponent = jnp.exp(scores - highest)
    total = jnp.sum(exponent, axis=-1, keepdims=True)
    weighted = jnp.dot(exponent.astype(BF16), values, preferred_element_type=F32)
    return highest, total, weighted


def kernel(
    shards, cap, groups, plan,
    cache, evicted, weight, target, counts, queries, fresh,
    merged, attended,
    evict_v, weight_v, target_v, counts_v, query_v, fresh_v,
    send, recv, meta_send, meta_recv, query_s, fresh_o, fresh_ml,
    part, part_m, part_recv, part_m_recv, shared, shared_m, result,
    in_sem, cache_sem, row_ssem, row_rsem, meta_sem,
    part_ssem, part_rsem, share_ssem, share_rsem, res_ssem, res_rsem,
):
    reqs, heads, kept, width = merged.shape
    pairs = reqs * heads
    evict = evict_v.shape[2]
    steps, _, _, depth = query_v.shape
    rows = query_s.shape[1]
    group = rows // steps
    slots = shards * cap
    scale = 1.0 / math.sqrt(depth)
    me = lax.axis_index("seq")
    core = lax.axis_index("hd")

    def peer(d):
        return lax.rem(me + d, shards)

    def source(d):
        return lax.rem(me + shards - d, shards)

    def remote(src, dst, ssem, rsem, device):
        return pltpu.make_async_remote_copy(
            src_ref=src, dst_ref=dst, send_sem=ssem, recv_sem=rsem,
            device_id={"seq": device}, device_id_type=pl.DeviceIdType.MESH,
        )

    small = [
        pltpu.make_async_copy(src, dst, in_sem.at[i])
        for i, (src, dst) in enumerate((
            (target, target_v), (weight, weight_v), (evicted, evict_v),
            (queries, query_v), (fresh, fresh_v), (counts, counts_v),
        ))
    ]
    for copy in small:
        copy.start()
    load = pltpu.make_async_copy(cache, merged, cache_sem.at[0])
    load.start()

    barrier = pltpu.get_barrier_semaphore()
    for d in range(1, shards):
        pl.semaphore_signal(
            barrier, inc=1, device_id={"seq": peer(d)}, device_id_type=pl.DeviceIdType.MESH
        )

    diagonal = lax.broadcasted_iota(jnp.int32, (rows, 128), 0) == lax.broadcasted_iota(
        jnp.int32, (rows, 128), 1
    )

    def to_rows(*columns):
        flat = [jnp.sum(jnp.where(diagonal, c, 0.0), axis=0, keepdims=True) for c in columns]
        return jnp.concatenate(flat, axis=0)

    def to_column(row):
        return jnp.sum(jnp.where(diagonal, row, 0.0), axis=1, keepdims=True)

    def attend_new():
        padded = -(-steps // 16) * 16
        new_step = lax.broadcasted_iota(jnp.int32, (rows, padded), 1)
        row_index = lax.broadcasted_iota(jnp.int32, (rows, padded), 0)
        allowed = row_index < 0
        for s in range(steps):
            allowed = allowed | ((new_step == s) & (row_index >= s * group))
        for r in range(reqs):
            asked = [query_v[s, r].astype(F32) for s in range(steps)]
            added = [fresh_v[s, r].astype(F32) for s in range(steps)]
            for h in range(heads):
                i = r * heads + h
                query = jnp.concatenate(
                    [a[h * group : (h + 1) * group] for a in asked], axis=0
                ).astype(BF16)
                query_s[i] = query
                latest = jnp.concatenate(
                    [a[h : h + 1] for a in added] + [jnp.zeros((padded - steps, width), F32)],
                    axis=0,
                ).astype(BF16)
                highest, total, weighted = softmax_block(
                    query, latest[:, :depth], latest[:, depth:], allowed, scale
                )
                fresh_o[i] = weighted
                fresh_ml[i, 0:2, :] = to_rows(highest, total)

    for copy in small[3:]:
        copy.wait()

    @pl.when(core != 0)
    def _():
        attend_new()

    for copy in small[:3]:
        copy.wait()
    aimed = jnp.concatenate([target_v[r] for r in range(reqs)], axis=0)
    weights = jnp.concatenate([weight_v[r].astype(F32) for r in range(reqs)], axis=0)
    owned, position, base = [], jnp.zeros_like(aimed), jnp.zeros(aimed.shape, F32)
    for d in range(shards):
        low = peer(d) * kept
        mine = (aimed >= low) & (aimed < low + kept)
        owned.append(jnp.where(mine, 1.0, 0.0))
        position = jnp.where(mine, aimed - low, position)
        base = jnp.where(mine, float(d * cap), base)
    above = lax.broadcasted_iota(jnp.int32, (evict, evict), 0) < lax.broadcasted_iota(
        jnp.int32, (evict, evict), 1
    )
    earlier = jnp.dot(
        jnp.concatenate(owned, axis=0).astype(BF16),
        jnp.where(above, 1.0, 0.0).astype(BF16),
        preferred_element_type=F32,
    )
    slot = base
    for d in range(shards):
        slot = slot + owned[d] * earlier[d * pairs : (d + 1) * pairs]
    slot = slot.astype(jnp.int32)
    features = jnp.concatenate(
        [weights, (position & 255).astype(F32), (position >> 8).astype(F32)], axis=0
    ).astype(BF16)
    slot_row = lax.broadcasted_iota(jnp.int32, (slots, evict), 0)
    for i in range(pairs):
        r, h = divmod(i, heads)
        packing = jnp.where(slot_row == slot[i : i + 1, :], 1.0, 0.0).astype(BF16)
        packed = jnp.dot(packing, evict_v[r, h], preferred_element_type=F32).astype(BF16)
        send[i] = packed
        recv[i, 0:cap, :] = packed[0:cap]
        meta = contract_last(features, packing)
        meta_send[i : i + 1, :] = (
            (meta[2 * pairs + i : 2 * pairs + i + 1] * 256.0 + meta[pairs + i : pairs + i + 1])
            * 2048.0 + meta[i : i + 1] * 512.0
        )

    pl.semaphore_wait(barrier, shards - 1)

    others = pl.ds(1, shards - 1)

    def all_of(ref, ssem, rsem):
        return remote(ref, ref, ssem, rsem, peer(1))

    for d in range(1, shards):
        remote(meta_send, meta_recv.at[d], meta_sem.at[0], meta_sem.at[1], peer(d)).start()
    span = pairs // groups
    for g in range(groups):
        for d in range(1, shards):
            lot = (pl.ds(g * span, span), pl.ds(d * cap, cap))
            remote(send.at[lot], recv.at[lot], row_ssem.at[0], row_rsem.at[g], peer(d)).start()

    def rows_in(g):
        lot = (pl.ds(g * span, span), pl.ds(cap, slots - cap))
        return all_of(recv.at[lot], row_ssem.at[0], row_rsem.at[g])

    @pl.when(core == 0)
    def _():
        attend_new()

    meta_in = all_of(meta_recv.at[others], meta_sem.at[0], meta_sem.at[1])
    meta_in.wait_recv()
    lane = lax.broadcasted_iota(jnp.int32, (pairs, slots), 1)
    meta = meta_send[...]
    for d in range(1, shards):
        meta = jnp.where(lane >= d * cap, meta_recv[d], meta)
    slot_position = (meta * (1.0 / 2048.0)).astype(jnp.int32)
    slot_weight = (meta - slot_position.astype(F32) * 2048.0) * (1.0 / 512.0)

    kept_row = lax.broadcasted_iota(jnp.int32, (kept, slots), 0)
    kept_lane = lax.broadcasted_iota(jnp.int32, (rows, kept), 1)
    ones = jnp.ones((slots, 128), BF16)

    def merge(i):
        r, h = divmod(i, heads)
        if i == 0:
            load.wait()
        if i % span == 0:
            rows_in(i // span).wait_recv()
        placing = jnp.where(
            kept_row == slot_position[i : i + 1], slot_weight[i : i + 1], 0.0
        ).astype(BF16)
        summed = jnp.dot(placing, recv[i], preferred_element_type=F32)
        factor = 1.0 / (1.0 + jnp.dot(placing, ones, preferred_element_type=F32))
        factor = jnp.concatenate([factor] * (width // 128), axis=1)
        fused = ((merged[r, h].astype(F32) + summed) * factor).astype(BF16)
        merged[r, h] = fused
        return softmax_block(
            query_s[i], fused[:, :depth], fused[:, depth:], kept_lane < counts_v[:, r : r + 1], scale
        )

    def to_owner(k, count, owner):
        lot = pl.ds(0, count * rows)
        away = lax.rem(owner - me + shards, shards)
        return (
            remote(
                part.at[k, lot], part_recv.at[k, away, lot],
                part_ssem.at[k, 0], part_rsem.at[k, 0], owner,
            ),
            remote(
                part_m.at[k], part_m_recv.at[k, away],
                part_ssem.at[k, 1], part_rsem.at[k, 1], owner,
            ),
        )

    def parts_in(k, count):
        lot = pl.ds(0, count * rows)
        return (
            all_of(part_recv.at[k, others, lot], part_ssem.at[k, 0], part_rsem.at[k, 0]),
            all_of(part_m_recv.at[k, others], part_ssem.at[k, 1], part_rsem.at[k, 1]),
        )

    def share_rows(k, j, d):
        lot = shared.at[k, me, pl.ds(j * rows, rows)]
        return remote(lot, lot, share_ssem.at[k, 0], share_rsem.at[k, 0], peer(d))

    def share_tops(k, d):
        lot = shared_m.at[k, me]
        return remote(lot, lot, share_ssem.at[k, 1], share_rsem.at[k, 1], peer(d))

    def shares(k, count):
        lot = pl.ds(0, count * rows)
        return (
            all_of(shared.at[k, others, lot], share_ssem.at[k, 0], share_rsem.at[k, 0]),
            all_of(shared_m.at[k, others], share_ssem.at[k, 1], share_rsem.at[k, 1]),
        )

    def send_result(k, first, count, d):
        lot = result.at[pl.ds(first, count)]
        return remote(lot, lot, res_ssem.at[k], res_rsem.at[k], peer(d))

    owned_plan = [(k, *entry) for k, entry in enumerate(plan) if entry[2] is not None]
    owned_index = {entry[0]: n for n, entry in enumerate(owned_plan)}
    shared_plan = [(k, *entry) for k, entry in enumerate(plan) if entry[2] is None]
    shared_index = {entry[0]: n for n, entry in enumerate(shared_plan)}

    for k, (first, count, owner) in enumerate(plan):
        for j in range(count):
            highest, total, weighted = merge(first + j)
            size = jnp.maximum(jnp.max(jnp.abs(weighted), axis=-1, keepdims=True), 1e-30)
            coded = jnp.round(weighted * (32767.0 / size)).astype(jnp.int32).astype(jnp.int16)
            if owner is None:
                into, into_m = shared.at[shared_index[k], me], shared_m.at[shared_index[k], me]
            else:
                into, into_m = part.at[owned_index[k]], part_m.at[owned_index[k]]
            into[j * rows : (j + 1) * rows, :] = coded
            if owner is None:
                for d in range(1, shards):
                    share_rows(shared_index[k], j, d).start()
            into_m[3 * j : 3 * j + 3, :] = to_rows(highest, total, size * (1.0 / 32767.0))
        if owner is None:
            for d in range(1, shards):
                share_tops(shared_index[k], d).start()
        else:
            @pl.when(me != owner)
            def _():
                for copy in to_owner(owned_index[k], count, owner):
                    copy.start()

    lanes = lax.broadcasted_iota(jnp.int32, (1, 128), 1)

    def combine(first, count, blocks):
        for j in range(count):
            i = first + j
            tiles = [fresh_ml[i, 0:2, :]] + [m[3 * j : 3 * j + 3, :] for _, m in blocks]
            outs = [fresh_o[i]] + [
                b[j * rows : (j + 1) * rows, :].astype(jnp.int32).astype(F32) for b, _ in blocks
            ]
            top = tiles[0][0:1]
            for tile in tiles[1:]:
                top = jnp.maximum(top, tile[0:1])
            shares = [jnp.exp(tile[0:1] - top) for tile in tiles]
            total = shares[0] * tiles[0][1:2]
            for share, tile in zip(shares[1:], tiles[1:]):
                total = total + share * tile[1:2]
            total = jnp.where(lanes < rows, total, 1.0)
            blend = to_column(shares[0] / total) * outs[0]
            for share, tile, out in zip(shares[1:], tiles[1:], outs[1:]):
                blend = blend + to_column(share * tile[2:3] / total) * out
            result[i] = blend.astype(BF16)

    for k, first, count, owner in owned_plan:
        n = owned_index[k]

        @pl.when(me == owner)
        def _():
            for copy in parts_in(n, count):
                copy.wait_recv()
            combine(
                first, count,
                [(part.at[n], part_m.at[n])]
                + [(part_recv.at[n, d], part_m_recv.at[n, d]) for d in range(1, shards)],
            )
            for d in range(1, shards):
                send_result(n, first, count, d).start()

    for k, first, count, _ in shared_plan:
        n = shared_index[k]
        for copy in shares(n, count):
            copy.wait_recv()
        combine(first, count, [(shared.at[n, d], shared_m.at[n, d]) for d in range(shards)])

    for k, first, count, owner in owned_plan:
        @pl.when(me != owner)
        def _():
            send_result(owned_index[k], first, count, 1).wait_recv()

    for r in range(reqs):
        done = [result[r * heads + h].astype(F32) for h in range(heads)]
        for s in range(steps):
            attended[s, r] = jnp.concatenate(
                [a[s * group : (s + 1) * group] for a in done], axis=0
            ).astype(BF16)

    meta_in.wait_send()
    sent = (pl.ds(0, pairs), pl.ds(cap, slots - cap))
    all_of(recv.at[sent], row_ssem.at[0], row_rsem.at[0]).wait_send()
    for k, first, count, owner in owned_plan:
        n = owned_index[k]

        @pl.when(me != owner)
        def _():
            for copy in to_owner(n, count, owner):
                copy.wait_send()

        @pl.when(me == owner)
        def _():
            lot = part_recv.at[n, others, pl.ds(0, count * rows)]
            all_of(lot, res_ssem.at[n], res_rsem.at[n]).wait_send()

    for k, first, count, _ in shared_plan:
        for copy in shares(shared_index[k], count):
            copy.wait_send()


def write_out(merged, attended, merged_out, attended_out, sem):
    copies = [
        pltpu.make_async_copy(merged, merged_out, sem.at[0]),
        pltpu.make_async_copy(attended, attended_out, sem.at[1]),
    ]
    for copy in copies:
        copy.start()
    for copy in copies:
        copy.wait()


def schedule(shards, pairs):
    per = max(1, pairs // shards)
    firsts = list(range(0, pairs, per))
    late = len(firsts) // 2 if shards <= 8 else 0
    return tuple(
        (first, min(per, pairs - first), None)
        if n >= len(firsts) - late
        else (first, min(per, pairs - first), (shards // 2 - 1 + n) % shards)
        for n, first in enumerate(firsts)
    )


def body(shards, cache, evicted, merge_weight, targets, kept_counts, queries, new_rows):
    reqs, heads, kept, width = cache.shape
    pairs = reqs * heads
    evict = evicted.shape[2]
    steps, _, query_local, depth = queries.shape
    rows = steps * query_local // heads
    cap = -(-max(2, 2 * evict // shards) // 16) * 16
    slots = shards * cap
    groups = pairs if shards <= 8 else 1
    plan = schedule(shards, pairs)
    most = max(count for _, count, _ in plan)
    owned = max(1, sum(owner is not None for _, _, owner in plan))
    common = max(1, len(plan) - owned)
    high = -(-3 * most // 8) * 8
    dma = pltpu.SemaphoreType.DMA
    done = pl.pallas_call(
        functools.partial(kernel, shards, cap, groups, plan),
        out_shape=(
            jax.ShapeDtypeStruct(cache.shape, BF16),
            jax.ShapeDtypeStruct(queries.shape, BF16),
        ),
        in_specs=[pl.BlockSpec(memory_space=pltpu.HBM)] * 7,
        out_specs=(pl.BlockSpec(memory_space=pltpu.VMEM),) * 2,
        scratch_shapes=[
            pltpu.VMEM(evicted.shape, BF16),
            pltpu.VMEM(merge_weight.shape, BF16),
            pltpu.VMEM(targets.shape, jnp.int32),
            pltpu.VMEM(kept_counts.shape[::-1], jnp.int32),
            pltpu.VMEM(queries.shape, BF16),
            pltpu.VMEM(new_rows.shape, BF16),
            pltpu.VMEM((pairs, slots, width), BF16),
            pltpu.VMEM((pairs, slots, width), BF16),
            pltpu.VMEM((pairs, slots), F32),
            pltpu.VMEM((shards, pairs, slots), F32),
            pltpu.VMEM((pairs, rows, depth), BF16),
            pltpu.VMEM((pairs, rows, depth), F32),
            pltpu.VMEM((pairs, 8, 128), F32),
            pltpu.VMEM((owned, most * rows, depth), jnp.int16),
            pltpu.VMEM((owned, high, 128), F32),
            pltpu.VMEM((owned, shards, most * rows, depth), jnp.int16),
            pltpu.VMEM((owned, shards, high, 128), F32),
            pltpu.VMEM((common, shards, most * rows, depth), jnp.int16),
            pltpu.VMEM((common, shards, high, 128), F32),
            pltpu.VMEM((pairs, rows, depth), BF16),
            dma((6,)),
            dma((1,)),
            dma((1,)),
            dma((groups,)),
            dma((2,)),
            dma((owned, 2)),
            dma((owned, 2)),
            dma((common, 2)),
            dma((common, 2)),
            dma((owned,)),
            dma((owned,)),
        ],
        compiler_params=pltpu.CompilerParams(
            collective_id=0, has_side_effects=True, vmem_limit_bytes=48 * 1024 * 1024
        ),
    )(*(
        pltpu.with_memory_space_constraint(a, pltpu.HBM)
        for a in (cache, evicted, merge_weight, targets, kept_counts.T, queries, new_rows)
    ))
    return pl.pallas_call(
        write_out,
        out_shape=tuple(jax.ShapeDtypeStruct(a.shape, a.dtype) for a in done),
        in_specs=[pl.BlockSpec(memory_space=pltpu.VMEM)] * 2,
        out_specs=(pl.BlockSpec(memory_space=pltpu.HBM),) * 2,
        scratch_shapes=[dma((2,))],
    )(*(pltpu.with_memory_space_constraint(a, pltpu.VMEM) for a in done))


def solution(mesh):
    return jax.shard_map(
        functools.partial(body, mesh.shape["seq"]),
        mesh=mesh,
        in_specs=(
            P(("grp", "req"), "hd", "seq", None),
            P(("grp", "req"), "hd", "seq", None),
            P(("grp", "req"), "hd", "seq"),
            P(("grp", "req"), "hd", "seq"),
            P(("grp", "req"), "seq"),
            P(None, ("grp", "req"), "hd", None),
            P(None, ("grp", "req"), "hd", None),
        ),
        out_specs=(P(("grp", "req"), "hd", "seq", None), P(None, ("grp", "req"), "hd", None)),
        check_vma=False,
    )
```

```python
import functools
import math

import jax
import jax.numpy as jnp
from jax import lax
from jax.experimental import pallas as pl
from jax.experimental.pallas import tpu as pltpu
from jax.sharding import PartitionSpec as P

F32 = jnp.float32
BF16 = jnp.bfloat16
NEG = -1e30


def contract_last(a, b):
    return lax.dot_general(a, b, (((1,), (1,)), ((), ())), preferred_element_type=F32)


def softmax_block(query, keys, values, allowed, scale):
    scores = jnp.where(allowed, contract_last(query, keys) * scale, NEG)
    highest = jnp.max(scores, axis=-1, keepdims=True)
    exponent = jnp.exp(scores - highest)
    total = jnp.sum(exponent, axis=-1, keepdims=True)
    weighted = jnp.dot(exponent.astype(BF16), values, preferred_element_type=F32)
    return highest, total, weighted


def kernel(
    shards, cap, chunks, plan,
    cache, evicted, weight, target, counts, queries, fresh,
    merged, attended,
    evict_v, weight_v, target_v, counts_v, query_v, fresh_v,
    send, recv, meta_send, meta_recv, query_s, fresh_o, fresh_ml,
    part, part_m, part_recv, part_m_recv, shared, shared_m, result,
    near_sem, in_sem, cache_sem, row_ssem, row_rsem, meta_sem,
    part_ssem, part_rsem, share_ssem, share_rsem, res_ssem, res_rsem,
):
    reqs, heads, kept, width = merged.shape
    pairs = reqs * heads
    evict = evict_v.shape[2]
    steps, _, _, depth = query_v.shape
    rows = query_s.shape[1]
    group = rows // steps
    slots = shards * cap
    scale = 1.0 / math.sqrt(depth)
    me = lax.axis_index("seq")
    core = lax.axis_index("hd")

    def peer(d):
        return lax.rem(me + d, shards)

    def source(d):
        return lax.rem(me + shards - d, shards)

    def remote(src, dst, ssem, rsem, device):
        return pltpu.make_async_remote_copy(
            src_ref=src, dst_ref=dst, send_sem=ssem, recv_sem=rsem,
            device_id={"seq": device}, device_id_type=pl.DeviceIdType.MESH,
        )

    small = [
        pltpu.make_async_copy(src, dst, in_sem.at[i])
        for i, (src, dst) in enumerate((
            (target, target_v), (weight, weight_v), (evicted, evict_v),
            (queries, query_v), (fresh, fresh_v), (counts, counts_v),
        ))
    ]
    for copy in small:
        copy.start()
    load = pltpu.make_async_copy(cache, merged, cache_sem.at[0])
    load.start()

    def tell(sem, device):
        pl.semaphore_signal(
            sem, inc=1, device_id={"seq": device}, device_id_type=pl.DeviceIdType.MESH
        )

    chain = len(chunks) > 1
    barrier = pltpu.get_barrier_semaphore()
    if chain:
        @pl.when(me > 0)
        def _():
            tell(barrier, me - 1)

        @pl.when(me < shards - 1)
        def _():
            tell(barrier, me + 1)
    else:
        for d in range(1, shards):
            tell(barrier, peer(d))

    diagonal = lax.broadcasted_iota(jnp.int32, (rows, 128), 0) == lax.broadcasted_iota(
        jnp.int32, (rows, 128), 1
    )

    def to_rows(*columns):
        flat = [jnp.sum(jnp.where(diagonal, c, 0.0), axis=0, keepdims=True) for c in columns]
        return jnp.concatenate(flat, axis=0)

    def to_column(row):
        return jnp.sum(jnp.where(diagonal, row, 0.0), axis=1, keepdims=True)

    def attend_new():
        padded = -(-steps // 16) * 16
        new_step = lax.broadcasted_iota(jnp.int32, (rows, padded), 1)
        row_index = lax.broadcasted_iota(jnp.int32, (rows, padded), 0)
        allowed = row_index < 0
        for s in range(steps):
            allowed = allowed | ((new_step == s) & (row_index >= s * group))
        for r in range(reqs):
            asked = [query_v[s, r].astype(F32) for s in range(steps)]
            added = [fresh_v[s, r].astype(F32) for s in range(steps)]
            for h in range(heads):
                i = r * heads + h
                query = jnp.concatenate(
                    [a[h * group : (h + 1) * group] for a in asked], axis=0
                ).astype(BF16)
                query_s[i] = query
                latest = jnp.concatenate(
                    [a[h : h + 1] for a in added] + [jnp.zeros((padded - steps, width), F32)],
                    axis=0,
                ).astype(BF16)
                highest, total, weighted = softmax_block(
                    query, latest[:, :depth], latest[:, depth:], allowed, scale
                )
                fresh_o[i] = weighted
                fresh_ml[i, 0:2, :] = to_rows(highest, total)

    for copy in small[3:]:
        copy.wait()

    @pl.when(core != 0)
    def _():
        attend_new()

    for copy in small[:3]:
        copy.wait()
    aimed = jnp.concatenate([target_v[r] for r in range(reqs)], axis=0)
    weights = jnp.concatenate([weight_v[r].astype(F32) for r in range(reqs)], axis=0)
    owned, position, base = [], jnp.zeros_like(aimed), jnp.zeros(aimed.shape, F32)
    for d in range(shards):
        low = peer(d) * kept
        mine = (aimed >= low) & (aimed < low + kept)
        owned.append(jnp.where(mine, 1.0, 0.0))
        position = jnp.where(mine, aimed - low, position)
        base = jnp.where(mine, float(d * cap), base)
    above = lax.broadcasted_iota(jnp.int32, (evict, evict), 0) < lax.broadcasted_iota(
        jnp.int32, (evict, evict), 1
    )
    earlier = jnp.dot(
        jnp.concatenate(owned, axis=0).astype(BF16),
        jnp.where(above, 1.0, 0.0).astype(BF16),
        preferred_element_type=F32,
    )
    slot = base
    for d in range(shards):
        slot = slot + owned[d] * earlier[d * pairs : (d + 1) * pairs]
    slot = slot.astype(jnp.int32)
    features = jnp.concatenate(
        [weights, (position & 255).astype(F32), (position >> 8).astype(F32)], axis=0
    ).astype(BF16)
    slot_row = lax.broadcasted_iota(jnp.int32, (slots, evict), 0)

    def pack(i):
        r, h = divmod(i, heads)
        packing = jnp.where(slot_row == slot[i : i + 1, :], 1.0, 0.0).astype(BF16)
        packed = jnp.dot(packing, evict_v[r, h], preferred_element_type=F32).astype(BF16)
        send[i] = packed
        recv[i, 0:cap, :] = packed[0:cap]
        meta = contract_last(features, packing)
        meta_send[i : i + 1, :] = (
            (meta[2 * pairs + i : 2 * pairs + i + 1] * 256.0 + meta[pairs + i : pairs + i + 1])
            * 2048.0 + meta[i : i + 1] * 512.0
        )

    others = pl.ds(1, shards - 1)

    def all_of(ref, ssem, rsem):
        return remote(ref, ref, ssem, rsem, peer(1))

    def send_rows(c, d):
        first, count = chunks[c]
        lot = (pl.ds(first, count), pl.ds(d * cap, cap))
        remote(send.at[lot], recv.at[lot], row_ssem.at[0], row_rsem.at[c], peer(d)).start()

    def send_meta(d):
        remote(meta_send, meta_recv.at[d], meta_sem.at[0], meta_sem.at[1], peer(d)).start()

    def rows_in(c):
        first, count = chunks[c]
        lot = (pl.ds(first, count), pl.ds(cap, slots - cap))
        return all_of(recv.at[lot], row_ssem.at[0], row_rsem.at[c])

    def send_rest(m):
        there = sorted((t for t in range(shards) if t != m), key=lambda t: -abs(t - m))
        edge = m in (0, shards - 1)
        for c in range(1, len(chunks)):
            for t in there[:-1] if edge else there:
                send_rows(c, (t - m) % shards)
        if edge:
            for c in range(1, len(chunks)):
                send_rows(c, (there[-1] - m) % shards)

    for i in range(chunks[0][1]):
        pack(i)

    if chain:
        inner = (me > 0) & (me < shards - 1)

        @pl.when(jnp.logical_not(inner))
        def _():
            pl.semaphore_wait(barrier, 1)

        @pl.when(inner)
        def _():
            pl.semaphore_wait(barrier, 2)
            tell(near_sem.at[0, 0], me - 1)
            tell(near_sem.at[1, 0], me + 1)

        @pl.when(me < shards - 1)
        def _():
            send_rows(0, 1)

        @pl.when(me > 0)
        def _():
            send_rows(0, shards - 1)

    for i in range(chunks[0][1], pairs):
        pack(i)

    if chain:
        @pl.when(core == 0)
        def _():
            attend_new()

        for m in range(shards):
            @pl.when(me == m)
            def _():
                for far in range(2, shards):
                    if m + far < shards:
                        pl.semaphore_wait(near_sem.at[0, far - 2], 1)
                        if m > 0:
                            tell(near_sem.at[0, far - 1], m - 1)
                        send_rows(0, far)
                    if m - far >= 0:
                        pl.semaphore_wait(near_sem.at[1, far - 2], 1)
                        if m < shards - 1:
                            tell(near_sem.at[1, far - 1], m + 1)
                        send_rows(0, shards - far)
                there = sorted((t for t in range(shards) if t != m), key=lambda t: -abs(t - m))
                for t in there:
                    send_meta((t - m) % shards)

                @pl.when(core == 0)
                def _():
                    send_rest(m)
    else:
        pl.semaphore_wait(barrier, shards - 1)
        for d in range(1, shards):
            send_meta(d)
        for c in range(len(chunks)):
            for d in range(1, shards):
                send_rows(c, d)

        @pl.when(core == 0)
        def _():
            attend_new()

    meta_in = all_of(meta_recv.at[others], meta_sem.at[0], meta_sem.at[1])
    meta_in.wait_recv()
    lane = lax.broadcasted_iota(jnp.int32, (pairs, slots), 1)
    meta = meta_send[...]
    for d in range(1, shards):
        meta = jnp.where(lane >= d * cap, meta_recv[d], meta)
    slot_position = (meta * (1.0 / 2048.0)).astype(jnp.int32)
    slot_weight = (meta - slot_position.astype(F32) * 2048.0) * (1.0 / 512.0)

    kept_row = lax.broadcasted_iota(jnp.int32, (kept, slots), 0)
    kept_lane = lax.broadcasted_iota(jnp.int32, (rows, kept), 1)
    ones = jnp.ones((slots, 128), BF16)

    def merge(i):
        r, h = divmod(i, heads)
        placing = jnp.where(
            kept_row == slot_position[i : i + 1], slot_weight[i : i + 1], 0.0
        ).astype(BF16)
        factor = 1.0 / (1.0 + jnp.dot(placing, ones, preferred_element_type=F32))
        if i == 0:
            load.wait()
        for c, (first, _) in enumerate(chunks):
            if first == i:
                rows_in(c).wait_recv()
        if chain and i == 0:
            for m in range(shards):
                @pl.when((me == m) & (core != 0))
                def _():
                    send_rest(m)
        summed = jnp.dot(placing, recv[i], preferred_element_type=F32)
        factor = jnp.concatenate([factor] * (width // 128), axis=1)
        fused = ((merged[r, h].astype(F32) + summed) * factor).astype(BF16)
        merged[r, h] = fused
        return softmax_block(
            query_s[i], fused[:, :depth], fused[:, depth:], kept_lane < counts_v[:, r : r + 1], scale
        )

    def to_owner(k, count, owner):
        lot = pl.ds(0, count * rows)
        away = lax.rem(owner - me + shards, shards)
        return (
            remote(
                part.at[k, lot], part_recv.at[0, away, lot],
                part_ssem.at[k, 0], part_rsem.at[0, 0], owner,
            ),
            remote(
                part_m.at[k], part_m_recv.at[0, away],
                part_ssem.at[k, 1], part_rsem.at[0, 1], owner,
            ),
        )

    def parts_in(k, count):
        lot = pl.ds(0, count * rows)
        return (
            all_of(part_recv.at[0, others, lot], part_ssem.at[k, 0], part_rsem.at[0, 0]),
            all_of(part_m_recv.at[0, others], part_ssem.at[k, 1], part_rsem.at[0, 1]),
        )

    def share_rows(k, j, d):
        lot = shared.at[k, me, pl.ds(j * rows, rows)]
        return remote(lot, lot, share_ssem.at[k, 0], share_rsem.at[k, 0], peer(d))

    def share_tops(k, d):
        lot = shared_m.at[k, me]
        return remote(lot, lot, share_ssem.at[k, 1], share_rsem.at[k, 1], peer(d))

    def shares(k, count):
        lot = pl.ds(0, count * rows)
        return (
            all_of(shared.at[k, others, lot], share_ssem.at[k, 0], share_rsem.at[k, 0]),
            all_of(shared_m.at[k, others], share_ssem.at[k, 1], share_rsem.at[k, 1]),
        )

    def send_result(k, first, count, d):
        lot = result.at[pl.ds(first, count)]
        return remote(lot, lot, res_ssem.at[0], res_rsem.at[k], peer(d))

    owned_plan = [(k, *entry) for k, entry in enumerate(plan) if entry[2] is not None]
    owned_index = {entry[0]: n for n, entry in enumerate(owned_plan)}
    shared_plan = [(k, *entry) for k, entry in enumerate(plan) if entry[2] is None]
    shared_index = {entry[0]: n for n, entry in enumerate(shared_plan)}

    for k, (first, count, owner) in enumerate(plan):
        for j in range(count):
            highest, total, weighted = merge(first + j)
            size = jnp.maximum(jnp.max(jnp.abs(weighted), axis=-1, keepdims=True), 1e-30)
            coded = jnp.round(weighted * (32767.0 / size)).astype(jnp.int32).astype(jnp.int16)
            if owner is None:
                into, into_m = shared.at[shared_index[k], me], shared_m.at[shared_index[k], me]
            else:
                into, into_m = part.at[owned_index[k]], part_m.at[owned_index[k]]
            into[j * rows : (j + 1) * rows, :] = coded
            if owner is None:
                for d in range(1, shards):
                    share_rows(shared_index[k], j, d).start()
            into_m[3 * j : 3 * j + 3, :] = to_rows(highest, total, size * (1.0 / 32767.0))
        if owner is None:
            for d in range(1, shards):
                share_tops(shared_index[k], d).start()
        else:
            @pl.when(me != owner)
            def _():
                for copy in to_owner(owned_index[k], count, owner):
                    copy.start()

    lanes = lax.broadcasted_iota(jnp.int32, (1, 128), 1)

    def combine(first, count, blocks):
        for j in range(count):
            i = first + j
            tiles = [fresh_ml[i, 0:2, :]] + [m[3 * j : 3 * j + 3, :] for _, m in blocks]
            outs = [fresh_o[i]] + [
                b[j * rows : (j + 1) * rows, :].astype(jnp.int32).astype(F32) for b, _ in blocks
            ]
            top = tiles[0][0:1]
            for tile in tiles[1:]:
                top = jnp.maximum(top, tile[0:1])
            shares = [jnp.exp(tile[0:1] - top) for tile in tiles]
            total = shares[0] * tiles[0][1:2]
            for share, tile in zip(shares[1:], tiles[1:]):
                total = total + share * tile[1:2]
            total = jnp.where(lanes < rows, total, 1.0)
            blend = to_column(shares[0] / total) * outs[0]
            for share, tile, out in zip(shares[1:], tiles[1:], outs[1:]):
                blend = blend + to_column(share * tile[2:3] / total) * out
            result[i] = blend.astype(BF16)

    for k, first, count, owner in owned_plan:
        n = owned_index[k]

        @pl.when(me == owner)
        def _():
            for copy in parts_in(n, count):
                copy.wait_recv()
            combine(
                first, count,
                [(part.at[n], part_m.at[n])]
                + [(part_recv.at[0, d], part_m_recv.at[0, d]) for d in range(1, shards)],
            )
            for d in range(1, shards):
                send_result(n, first, count, d).start()

    for k, first, count, _ in shared_plan:
        n = shared_index[k]
        for copy in shares(n, count):
            copy.wait_recv()
        combine(first, count, [(shared.at[n, d], shared_m.at[n, d]) for d in range(shards)])

    for k, first, count, owner in owned_plan:
        @pl.when(me != owner)
        def _():
            send_result(owned_index[k], first, count, 1).wait_recv()

    for r in range(reqs):
        done = [result[r * heads + h].astype(F32) for h in range(heads)]
        for s in range(steps):
            attended[s, r] = jnp.concatenate(
                [a[s * group : (s + 1) * group] for a in done], axis=0
            ).astype(BF16)

    meta_in.wait_send()
    sent = (pl.ds(0, pairs), pl.ds(cap, slots - cap))
    all_of(recv.at[sent], row_ssem.at[0], row_rsem.at[0]).wait_send()
    for k, first, count, owner in owned_plan:
        n = owned_index[k]

        @pl.when(me != owner)
        def _():
            for copy in to_owner(n, count, owner):
                copy.wait_send()

        @pl.when(me == owner)
        def _():
            lot = part_recv.at[0, others, pl.ds(0, count * rows)]
            all_of(lot, res_ssem.at[0], res_rsem.at[n]).wait_send()

    for k, first, count, _ in shared_plan:
        for copy in shares(shared_index[k], count):
            copy.wait_send()


def write_out(merged, attended, merged_out, attended_out, sem):
    copies = [
        pltpu.make_async_copy(merged, merged_out, sem.at[0]),
        pltpu.make_async_copy(attended, attended_out, sem.at[1]),
    ]
    for copy in copies:
        copy.start()
    for copy in copies:
        copy.wait()


def schedule(shards, pairs):
    per = max(1, pairs // shards)
    firsts = list(range(0, pairs, per))
    owners = [(shards - 2 - n) % shards if shards <= 8 else n % shards for n in range(len(firsts))]
    if shards <= 8:
        owners[-1] = None
    return tuple((f, min(per, pairs - f), owner) for f, owner in zip(firsts, owners))


def row_chunks(shards, pairs):
    if shards > 8 or shards < 3:
        return ((0, pairs),)
    head = max(1, 3 * pairs // 8)
    return ((0, head),) + tuple((i, 1) for i in range(head, pairs))


def body(shards, cache, evicted, merge_weight, targets, kept_counts, queries, new_rows):
    reqs, heads, kept, width = cache.shape
    pairs = reqs * heads
    evict = evicted.shape[2]
    steps, _, query_local, depth = queries.shape
    rows = steps * query_local // heads
    cap = -(-max(2, 2 * evict // shards) // 16) * 16
    slots = shards * cap
    chunks = row_chunks(shards, pairs)
    plan = schedule(shards, pairs)
    most = max(count for _, count, _ in plan)
    owned = max(1, sum(owner is not None for _, _, owner in plan))
    common = max(1, len(plan) - owned)
    high = -(-3 * most // 8) * 8
    dma = pltpu.SemaphoreType.DMA
    done = pl.pallas_call(
        functools.partial(kernel, shards, cap, chunks, plan),
        out_shape=(
            jax.ShapeDtypeStruct(cache.shape, BF16),
            jax.ShapeDtypeStruct(queries.shape, BF16),
        ),
        in_specs=[pl.BlockSpec(memory_space=pltpu.HBM)] * 7,
        out_specs=(pl.BlockSpec(memory_space=pltpu.VMEM),) * 2,
        scratch_shapes=[
            pltpu.VMEM(evicted.shape, BF16),
            pltpu.VMEM(merge_weight.shape, BF16),
            pltpu.VMEM(targets.shape, jnp.int32),
            pltpu.VMEM(kept_counts.shape[::-1], jnp.int32),
            pltpu.VMEM(queries.shape, BF16),
            pltpu.VMEM(new_rows.shape, BF16),
            pltpu.VMEM((pairs, slots, width), BF16),
            pltpu.VMEM((pairs, slots, width), BF16),
            pltpu.VMEM((pairs, slots), F32),
            pltpu.VMEM((shards, pairs, slots), F32),
            pltpu.VMEM((pairs, rows, depth), BF16),
            pltpu.VMEM((pairs, rows, depth), F32),
            pltpu.VMEM((pairs, 8, 128), F32),
            pltpu.VMEM((owned, most * rows, depth), jnp.int16),
            pltpu.VMEM((owned, high, 128), F32),
            pltpu.VMEM((1, shards, most * rows, depth), jnp.int16),
            pltpu.VMEM((1, shards, high, 128), F32),
            pltpu.VMEM((common, shards, most * rows, depth), jnp.int16),
            pltpu.VMEM((common, shards, high, 128), F32),
            pltpu.VMEM((pairs, rows, depth), BF16),
            pltpu.SemaphoreType.REGULAR((2, max(1, shards - 2))),
            dma((6,)),
            dma((1,)),
            dma((1,)),
            dma((len(chunks),)),
            dma((2,)),
            dma((owned, 2)),
            dma((1, 2)),
            dma((common, 2)),
            dma((common, 2)),
            dma((1,)),
            dma((owned,)),
        ],
        compiler_params=pltpu.CompilerParams(
            collective_id=0, has_side_effects=True, vmem_limit_bytes=48 * 1024 * 1024
        ),
    )(*(
        pltpu.with_memory_space_constraint(a, pltpu.HBM)
        for a in (cache, evicted, merge_weight, targets, kept_counts.T, queries, new_rows)
    ))
    return pl.pallas_call(
        write_out,
        out_shape=tuple(jax.ShapeDtypeStruct(a.shape, a.dtype) for a in done),
        in_specs=[pl.BlockSpec(memory_space=pltpu.VMEM)] * 2,
        out_specs=(pl.BlockSpec(memory_space=pltpu.HBM),) * 2,
        scratch_shapes=[dma((2,))],
    )(*(pltpu.with_memory_space_constraint(a, pltpu.VMEM) for a in done))


def solution(mesh):
    return jax.shard_map(
        functools.partial(body, mesh.shape["seq"]),
        mesh=mesh,
        in_specs=(
            P(("grp", "req"), "hd", "seq", None),
            P(("grp", "req"), "hd", "seq", None),
            P(("grp", "req"), "hd", "seq"),
            P(("grp", "req"), "hd", "seq"),
            P(("grp", "req"), "seq"),
            P(None, ("grp", "req"), "hd", None),
            P(None, ("grp", "req"), "hd", None),
        ),
        out_specs=(P(("grp", "req"), "hd", "seq", None), P(None, ("grp", "req"), "hd", None)),
        check_vma=False,
    )
```

```python
import functools
import math

import jax
import jax.numpy as jnp
from jax import lax
from jax.experimental import pallas as pl
from jax.experimental.pallas import tpu as pltpu
from jax.sharding import PartitionSpec as P

F32 = jnp.float32
BF16 = jnp.bfloat16
NEG = -1e30


def contract_last(a, b):
    return lax.dot_general(a, b, (((1,), (1,)), ((), ())), preferred_element_type=F32)


def softmax_block(query, keys, values, allowed, scale):
    scores = jnp.where(allowed, contract_last(query, keys) * scale, NEG)
    highest = jnp.max(scores, axis=-1, keepdims=True)
    exponent = jnp.exp(scores - highest)
    total = jnp.sum(exponent, axis=-1, keepdims=True)
    weighted = jnp.dot(exponent.astype(BF16), values, preferred_element_type=F32)
    return highest, total, weighted


def kernel(
    shards, cap, chunks, plan,
    cache, evicted, weight, target, counts, queries, fresh,
    merged, attended,
    evict_v, weight_v, target_v, counts_v, query_v, fresh_v,
    send, recv, meta_send, meta_recv, query_s, fresh_o, fresh_ml,
    part, part_m, part_recv, part_m_recv, shared, shared_m, result,
    near_sem, in_sem, cache_sem, row_ssem, row_rsem, meta_sem,
    part_ssem, part_rsem, share_ssem, share_rsem, res_ssem, res_rsem,
):
    reqs, heads, kept, width = merged.shape
    pairs = reqs * heads
    evict = evict_v.shape[2]
    steps, _, _, depth = query_v.shape
    rows = query_s.shape[1]
    group = rows // steps
    slots = shards * cap
    scale = 1.0 / math.sqrt(depth)
    me = lax.axis_index("seq")
    core = lax.axis_index("hd")

    def peer(d):
        return lax.rem(me + d, shards)

    def source(d):
        return lax.rem(me + shards - d, shards)

    def remote(src, dst, ssem, rsem, device):
        return pltpu.make_async_remote_copy(
            src_ref=src, dst_ref=dst, send_sem=ssem, recv_sem=rsem,
            device_id={"seq": device}, device_id_type=pl.DeviceIdType.MESH,
        )

    small = [
        pltpu.make_async_copy(src, dst, in_sem.at[i])
        for i, (src, dst) in enumerate((
            (target, target_v), (weight, weight_v), (evicted, evict_v),
            (queries, query_v), (fresh, fresh_v), (counts, counts_v),
        ))
    ]
    for copy in small:
        copy.start()
    load = pltpu.make_async_copy(cache, merged, cache_sem.at[0])
    load.start()

    def tell(sem, device):
        pl.semaphore_signal(
            sem, inc=1, device_id={"seq": device}, device_id_type=pl.DeviceIdType.MESH
        )

    chain = len(chunks) > 1
    barrier = pltpu.get_barrier_semaphore()
    if chain:
        @pl.when(me > 0)
        def _():
            tell(barrier, me - 1)

        @pl.when(me < shards - 1)
        def _():
            tell(barrier, me + 1)
    else:
        for d in range(1, shards):
            tell(barrier, peer(d))

    ahead = lax.broadcasted_iota(jnp.int32, (rows, 128), 1) - lax.broadcasted_iota(
        jnp.int32, (rows, 128), 0
    )
    spot = {first + j: j * rows for first, count, _ in plan for j in range(count)}

    def to_row(*placed):
        grid = jnp.zeros((rows, 128), F32)
        for column, at in placed:
            grid = jnp.where(ahead == at, column, grid)
        return jnp.sum(grid, axis=0, keepdims=True)

    def to_column(row, at):
        return jnp.sum(jnp.where(ahead == at, row, 0.0), axis=1, keepdims=True)

    def attend_new():
        padded = -(-steps // 16) * 16
        new_step = lax.broadcasted_iota(jnp.int32, (rows, padded), 1)
        row_index = lax.broadcasted_iota(jnp.int32, (rows, padded), 0)
        allowed = row_index < 0
        for s in range(steps):
            allowed = allowed | ((new_step == s) & (row_index >= s * group))
        for r in range(reqs):
            asked = [query_v[s, r].astype(F32) for s in range(steps)]
            added = [fresh_v[s, r].astype(F32) for s in range(steps)]
            for h in range(heads):
                i = r * heads + h
                query = jnp.concatenate(
                    [a[h * group : (h + 1) * group] for a in asked], axis=0
                ).astype(BF16)
                query_s[i] = query
                latest = jnp.concatenate(
                    [a[h : h + 1] for a in added] + [jnp.zeros((padded - steps, width), F32)],
                    axis=0,
                ).astype(BF16)
                highest, total, weighted = softmax_block(
                    query, latest[:, :depth], latest[:, depth:], allowed, scale
                )
                fresh_o[i] = weighted
                fresh_ml[i, 0:1, :] = to_row((highest, spot[i]))
                fresh_ml[i, 1:2, :] = to_row((total, spot[i]))

    for copy in small[3:]:
        copy.wait()

    @pl.when(core != 0)
    def _():
        attend_new()

    for copy in small[:3]:
        copy.wait()
    aimed = jnp.concatenate([target_v[r] for r in range(reqs)], axis=0)
    weights = jnp.concatenate([weight_v[r].astype(F32) for r in range(reqs)], axis=0)
    owned, position, base = [], jnp.zeros_like(aimed), jnp.zeros(aimed.shape, F32)
    for d in range(shards):
        low = peer(d) * kept
        mine = (aimed >= low) & (aimed < low + kept)
        owned.append(jnp.where(mine, 1.0, 0.0))
        position = jnp.where(mine, aimed - low, position)
        base = jnp.where(mine, float(d * cap), base)
    above = lax.broadcasted_iota(jnp.int32, (evict, evict), 0) < lax.broadcasted_iota(
        jnp.int32, (evict, evict), 1
    )
    earlier = jnp.dot(
        jnp.concatenate(owned, axis=0).astype(BF16),
        jnp.where(above, 1.0, 0.0).astype(BF16),
        preferred_element_type=F32,
    )
    slot = base
    for d in range(shards):
        slot = slot + owned[d] * earlier[d * pairs : (d + 1) * pairs]
    slot = slot.astype(jnp.int32)
    features = jnp.concatenate(
        [weights, (position & 255).astype(F32), (position >> 8).astype(F32)], axis=0
    ).astype(BF16)
    slot_row = lax.broadcasted_iota(jnp.int32, (slots, evict), 0)

    def pack(i):
        r, h = divmod(i, heads)
        packing = jnp.where(slot_row == slot[i : i + 1, :], 1.0, 0.0).astype(BF16)
        packed = jnp.dot(packing, evict_v[r, h], preferred_element_type=F32).astype(BF16)
        send[i] = packed
        recv[i, 0:cap, :] = packed[0:cap]
        meta = contract_last(features, packing)
        meta_send[i : i + 1, :] = (
            (meta[2 * pairs + i : 2 * pairs + i + 1] * 256.0 + meta[pairs + i : pairs + i + 1])
            * 2048.0 + meta[i : i + 1] * 512.0
        )

    others = pl.ds(1, shards - 1)

    def all_of(ref, ssem, rsem):
        return remote(ref, ref, ssem, rsem, peer(1))

    def send_rows(c, d):
        first, count = chunks[c]
        lot = (pl.ds(first, count), pl.ds(d * cap, cap))
        remote(send.at[lot], recv.at[lot], row_ssem.at[0], row_rsem.at[c], peer(d)).start()

    def send_meta(d):
        remote(meta_send, meta_recv.at[d], meta_sem.at[0], meta_sem.at[1], peer(d)).start()

    def rows_in(c):
        first, count = chunks[c]
        lot = (pl.ds(first, count), pl.ds(cap, slots - cap))
        return all_of(recv.at[lot], row_ssem.at[0], row_rsem.at[c])

    def send_rest(m):
        there = sorted((t for t in range(shards) if t != m), key=lambda t: -abs(t - m))
        edge = m in (0, shards - 1)
        for c in range(1, len(chunks)):
            for t in there[:-1] if edge else there:
                send_rows(c, (t - m) % shards)
        if edge:
            for c in range(1, len(chunks)):
                send_rows(c, (there[-1] - m) % shards)

    for i in range(chunks[0][1]):
        pack(i)

    if chain:
        inner = (me > 0) & (me < shards - 1)

        @pl.when(jnp.logical_not(inner))
        def _():
            pl.semaphore_wait(barrier, 1)

        @pl.when(inner)
        def _():
            pl.semaphore_wait(barrier, 2)
            tell(near_sem.at[0, 0], me - 1)
            tell(near_sem.at[1, 0], me + 1)

        @pl.when(me < shards - 1)
        def _():
            send_rows(0, 1)

        @pl.when(me > 0)
        def _():
            send_rows(0, shards - 1)

    for i in range(chunks[0][1], pairs):
        pack(i)

    if chain:
        @pl.when(core == 0)
        def _():
            attend_new()

        for m in range(shards):
            @pl.when(me == m)
            def _():
                for far in range(2, shards):
                    if m + far < shards:
                        pl.semaphore_wait(near_sem.at[0, far - 2], 1)
                        if m > 0:
                            tell(near_sem.at[0, far - 1], m - 1)
                        send_rows(0, far)
                    if m - far >= 0:
                        pl.semaphore_wait(near_sem.at[1, far - 2], 1)
                        if m < shards - 1:
                            tell(near_sem.at[1, far - 1], m + 1)
                        send_rows(0, shards - far)
                there = sorted((t for t in range(shards) if t != m), key=lambda t: -abs(t - m))
                for t in there:
                    send_meta((t - m) % shards)

                @pl.when(core == 0)
                def _():
                    send_rest(m)
    else:
        pl.semaphore_wait(barrier, shards - 1)
        for d in range(1, shards):
            send_meta(d)
        for c in range(len(chunks)):
            for d in range(1, shards):
                send_rows(c, d)

        @pl.when(core == 0)
        def _():
            attend_new()

    meta_in = all_of(meta_recv.at[others], meta_sem.at[0], meta_sem.at[1])
    meta_in.wait_recv()
    lane = lax.broadcasted_iota(jnp.int32, (pairs, slots), 1)
    meta = meta_send[...]
    for d in range(1, shards):
        meta = jnp.where(lane >= d * cap, meta_recv[d], meta)
    slot_position = (meta * (1.0 / 2048.0)).astype(jnp.int32)
    slot_weight = (meta - slot_position.astype(F32) * 2048.0) * (1.0 / 512.0)

    kept_row = lax.broadcasted_iota(jnp.int32, (kept, slots), 0).astype(jnp.int16)
    kept_lane = lax.broadcasted_iota(jnp.int32, (rows, kept), 1)
    ones = jnp.ones((slots, 128), BF16)

    def merge(i):
        r, h = divmod(i, heads)
        aims = jnp.broadcast_to(slot_position[i : i + 1], (16, slots)).astype(jnp.int16)
        gains = jnp.broadcast_to(slot_weight[i : i + 1], (16, slots)).astype(BF16)
        placing = jnp.where(
            kept_row == jnp.concatenate([aims] * (kept // 16), axis=0),
            jnp.concatenate([gains] * (kept // 16), axis=0),
            jnp.zeros((kept, slots), BF16),
        )
        factor = 1.0 / (1.0 + jnp.dot(placing, ones, preferred_element_type=F32))
        if i == 0:
            load.wait()
        for c, (first, _) in enumerate(chunks):
            if first == i:
                rows_in(c).wait_recv()
        if chain and i == 0:
            for m in range(shards):
                @pl.when((me == m) & (core != 0))
                def _():
                    send_rest(m)
        summed = jnp.dot(placing, recv[i], preferred_element_type=F32)
        factor = jnp.concatenate([factor] * (width // 128), axis=1)
        fused = ((merged[r, h].astype(F32) + summed) * factor).astype(BF16)
        merged[r, h] = fused
        return softmax_block(
            query_s[i], fused[:, :depth], fused[:, depth:], kept_lane < counts_v[:, r : r + 1], scale
        )

    def to_owner(k, count, owner):
        lot = pl.ds(0, count * rows)
        away = lax.rem(owner - me + shards, shards)
        return (
            remote(
                part.at[k, lot], part_recv.at[0, away, lot],
                part_ssem.at[k, 0], part_rsem.at[0, 0], owner,
            ),
            remote(
                part_m.at[k], part_m_recv.at[0, away],
                part_ssem.at[k, 1], part_rsem.at[0, 1], owner,
            ),
        )

    def parts_in(k, count):
        lot = pl.ds(0, count * rows)
        return (
            all_of(part_recv.at[0, others, lot], part_ssem.at[k, 0], part_rsem.at[0, 0]),
            all_of(part_m_recv.at[0, others], part_ssem.at[k, 1], part_rsem.at[0, 1]),
        )

    def share_rows(k, j, d):
        lot = shared.at[k, me, pl.ds(j * rows, rows)]
        return remote(lot, lot, share_ssem.at[k, 0], share_rsem.at[k, 0], peer(d))

    def share_tops(k, d):
        lot = shared_m.at[k, me]
        return remote(lot, lot, share_ssem.at[k, 1], share_rsem.at[k, 1], peer(d))

    def shares(k, count):
        lot = pl.ds(0, count * rows)
        return (
            all_of(shared.at[k, others, lot], share_ssem.at[k, 0], share_rsem.at[k, 0]),
            all_of(shared_m.at[k, others], share_ssem.at[k, 1], share_rsem.at[k, 1]),
        )

    def send_result(k, first, count, d):
        lot = result.at[pl.ds(first, count)]
        return remote(lot, lot, res_ssem.at[0], res_rsem.at[k], peer(d))

    owned_plan = [(k, *entry) for k, entry in enumerate(plan) if entry[2] is not None]
    owned_index = {entry[0]: n for n, entry in enumerate(owned_plan)}
    shared_plan = [(k, *entry) for k, entry in enumerate(plan) if entry[2] is None]
    shared_index = {entry[0]: n for n, entry in enumerate(shared_plan)}

    for k, (first, count, owner) in enumerate(plan):
        tops, sums = [], []
        for j in range(count):
            highest, total, weighted = merge(first + j)
            size = jnp.maximum(jnp.max(jnp.abs(weighted), axis=-1, keepdims=True), 1e-30)
            coded = jnp.round(weighted * (32767.0 / size)).astype(jnp.int32).astype(jnp.int16)
            if owner is None:
                into, into_m = shared.at[shared_index[k], me], shared_m.at[shared_index[k], me]
            else:
                into, into_m = part.at[owned_index[k]], part_m.at[owned_index[k]]
            into[j * rows : (j + 1) * rows, :] = coded
            if owner is None:
                for d in range(1, shards):
                    share_rows(shared_index[k], j, d).start()
            at = j * rows
            tops.append(to_row((highest, at), (size * (1.0 / 32767.0), at + 64)))
            sums.append(to_row((total, at)))
        into_m[0:1, :] = functools.reduce(jnp.add, tops)
        into_m[1:2, :] = functools.reduce(jnp.add, sums)
        if owner is None:
            for d in range(1, shards):
                share_tops(shared_index[k], d).start()
        else:
            @pl.when(me != owner)
            def _():
                for copy in to_owner(owned_index[k], count, owner):
                    copy.start()

    lanes = lax.broadcasted_iota(jnp.int32, (1, 128), 1)

    def combine(first, count, blocks):
        group = range(first, first + count)
        tiles = [
            (
                functools.reduce(jnp.add, [fresh_ml[i, 0:1, :] for i in group]),
                functools.reduce(jnp.add, [fresh_ml[i, 1:2, :] for i in group]),
            )
        ] + [(m[0:1, :], m[1:2, :]) for _, m in blocks]
        top = functools.reduce(jnp.maximum, [tile[0] for tile in tiles])
        shares = [jnp.exp(tile[0] - top) for tile in tiles]
        total = functools.reduce(jnp.add, [a * tile[1] for a, tile in zip(shares, tiles)])
        shares = [a / jnp.where(lanes < count * rows, total, 1.0) for a in shares]
        for n, (_, m) in enumerate(blocks):
            scales = jnp.concatenate([m[0:1, 64:], m[0:1, :64]], axis=1)
            shares[n + 1] = shares[n + 1] * scales
        for j, i in enumerate(group):
            blend = to_column(shares[0], j * rows) * fresh_o[i]
            for share, (b, _) in zip(shares[1:], blocks):
                out = b[j * rows : (j + 1) * rows, :].astype(jnp.int32).astype(F32)
                blend = blend + to_column(share, j * rows) * out
            result[i] = blend.astype(BF16)

    for k, first, count, owner in owned_plan:
        n = owned_index[k]

        @pl.when(me == owner)
        def _():
            for copy in parts_in(n, count):
                copy.wait_recv()
            combine(
                first, count,
                [(part.at[n], part_m.at[n])]
                + [(part_recv.at[0, d], part_m_recv.at[0, d]) for d in range(1, shards)],
            )
            for d in range(1, shards):
                send_result(n, first, count, d).start()

    for k, first, count, _ in shared_plan:
        n = shared_index[k]
        for copy in shares(n, count):
            copy.wait_recv()
        combine(first, count, [(shared.at[n, d], shared_m.at[n, d]) for d in range(shards)])

    for k, first, count, owner in owned_plan:
        @pl.when(me != owner)
        def _():
            send_result(owned_index[k], first, count, 1).wait_recv()

    for r in range(reqs):
        done = [result[r * heads + h].astype(F32) for h in range(heads)]
        for s in range(steps):
            attended[s, r] = jnp.concatenate(
                [a[s * group : (s + 1) * group] for a in done], axis=0
            ).astype(BF16)

    meta_in.wait_send()
    sent = (pl.ds(0, pairs), pl.ds(cap, slots - cap))
    all_of(recv.at[sent], row_ssem.at[0], row_rsem.at[0]).wait_send()
    for k, first, count, owner in owned_plan:
        n = owned_index[k]

        @pl.when(me != owner)
        def _():
            for copy in to_owner(n, count, owner):
                copy.wait_send()

        @pl.when(me == owner)
        def _():
            lot = part_recv.at[0, others, pl.ds(0, count * rows)]
            all_of(lot, res_ssem.at[0], res_rsem.at[n]).wait_send()

    for k, first, count, _ in shared_plan:
        for copy in shares(shared_index[k], count):
            copy.wait_send()


def write_out(merged, attended, merged_out, attended_out, sem):
    copies = [
        pltpu.make_async_copy(merged, merged_out, sem.at[0]),
        pltpu.make_async_copy(attended, attended_out, sem.at[1]),
    ]
    for copy in copies:
        copy.start()
    for copy in copies:
        copy.wait()


def schedule(shards, pairs):
    per = max(1, min(2, pairs // shards))
    firsts = list(range(0, pairs, per))
    owners = [(shards - 2 - n) % shards if shards <= 8 else n % shards for n in range(len(firsts))]
    if shards <= 8:
        owners[-1] = None
    return tuple((f, min(per, pairs - f), owner) for f, owner in zip(firsts, owners))


def row_chunks(shards, pairs):
    if shards > 8 or shards < 3:
        return ((0, pairs),)
    head = max(1, 3 * pairs // 8)
    return ((0, head),) + tuple((i, 1) for i in range(head, pairs))


def body(shards, cache, evicted, merge_weight, targets, kept_counts, queries, new_rows):
    reqs, heads, kept, width = cache.shape
    pairs = reqs * heads
    evict = evicted.shape[2]
    steps, _, query_local, depth = queries.shape
    rows = steps * query_local // heads
    cap = -(-max(2, 2 * evict // shards) // 16) * 16
    slots = shards * cap
    chunks = row_chunks(shards, pairs)
    plan = schedule(shards, pairs)
    most = max(count for _, count, _ in plan)
    owned = max(1, sum(owner is not None for _, _, owner in plan))
    common = max(1, len(plan) - owned)
    assert most * rows <= 64
    high = 2
    dma = pltpu.SemaphoreType.DMA
    done = pl.pallas_call(
        functools.partial(kernel, shards, cap, chunks, plan),
        out_shape=(
            jax.ShapeDtypeStruct(cache.shape, BF16),
            jax.ShapeDtypeStruct(queries.shape, BF16),
        ),
        in_specs=[pl.BlockSpec(memory_space=pltpu.HBM)] * 7,
        out_specs=(pl.BlockSpec(memory_space=pltpu.VMEM),) * 2,
        scratch_shapes=[
            pltpu.VMEM(evicted.shape, BF16),
            pltpu.VMEM(merge_weight.shape, BF16),
            pltpu.VMEM(targets.shape, jnp.int32),
            pltpu.VMEM(kept_counts.shape[::-1], jnp.int32),
            pltpu.VMEM(queries.shape, BF16),
            pltpu.VMEM(new_rows.shape, BF16),
            pltpu.VMEM((pairs, slots, width), BF16),
            pltpu.VMEM((pairs, slots, width), BF16),
            pltpu.VMEM((pairs, slots), F32),
            pltpu.VMEM((shards, pairs, slots), F32),
            pltpu.VMEM((pairs, rows, depth), BF16),
            pltpu.VMEM((pairs, rows, depth), F32),
            pltpu.VMEM((pairs, 2, 128), F32),
            pltpu.VMEM((owned, most * rows, depth), jnp.int16),
            pltpu.VMEM((owned, high, 128), F32),
            pltpu.VMEM((1, shards, most * rows, depth), jnp.int16),
            pltpu.VMEM((1, shards, high, 128), F32),
            pltpu.VMEM((common, shards, most * rows, depth), jnp.int16),
            pltpu.VMEM((common, shards, high, 128), F32),
            pltpu.VMEM((pairs, rows, depth), BF16),
            pltpu.SemaphoreType.REGULAR((2, max(1, shards - 2))),
            dma((6,)),
            dma((1,)),
            dma((1,)),
            dma((len(chunks),)),
            dma((2,)),
            dma((owned, 2)),
            dma((1, 2)),
            dma((common, 2)),
            dma((common, 2)),
            dma((1,)),
            dma((owned,)),
        ],
        compiler_params=pltpu.CompilerParams(
            collective_id=0, has_side_effects=True, vmem_limit_bytes=48 * 1024 * 1024
        ),
    )(*(
        pltpu.with_memory_space_constraint(a, pltpu.HBM)
        for a in (cache, evicted, merge_weight, targets, kept_counts.T, queries, new_rows)
    ))
    return pl.pallas_call(
        write_out,
        out_shape=tuple(jax.ShapeDtypeStruct(a.shape, a.dtype) for a in done),
        in_specs=[pl.BlockSpec(memory_space=pltpu.VMEM)] * 2,
        out_specs=(pl.BlockSpec(memory_space=pltpu.HBM),) * 2,
        scratch_shapes=[dma((2,))],
    )(*(pltpu.with_memory_space_constraint(a, pltpu.VMEM) for a in done))


def solution(mesh):
    return jax.shard_map(
        functools.partial(body, mesh.shape["seq"]),
        mesh=mesh,
        in_specs=(
            P(("grp", "req"), "hd", "seq", None),
            P(("grp", "req"), "hd", "seq", None),
            P(("grp", "req"), "hd", "seq"),
            P(("grp", "req"), "hd", "seq"),
            P(("grp", "req"), "seq"),
            P(None, ("grp", "req"), "hd", None),
            P(None, ("grp", "req"), "hd", None),
        ),
        out_specs=(P(("grp", "req"), "hd", "seq", None), P(None, ("grp", "req"), "hd", None)),
        check_vma=False,
    )
```

```python
import functools
import math

import jax
import jax.numpy as jnp
from jax import lax
from jax.experimental import pallas as pl
from jax.experimental.pallas import tpu as pltpu
from jax.sharding import PartitionSpec as P

F32 = jnp.float32
BF16 = jnp.bfloat16
NEG = -1e30


def contract_last(a, b):
    return lax.dot_general(a, b, (((1,), (1,)), ((), ())), preferred_element_type=F32)


def softmax_block(query, keys, values, allowed, scale):
    scores = jnp.where(allowed, contract_last(query, keys) * scale, NEG)
    highest = jnp.max(scores, axis=-1, keepdims=True)
    exponent = jnp.exp(scores - highest)
    total = jnp.sum(exponent, axis=-1, keepdims=True)
    weighted = jnp.dot(exponent.astype(BF16), values, preferred_element_type=F32)
    return highest, total, weighted


def kernel(
    shards, cap, chunks, plan,
    cache, evicted, weight, target, counts, queries, fresh,
    merged, attended,
    evict_v, weight_v, target_v, counts_v, query_v, fresh_v,
    send, recv, meta_send, meta_recv, query_s, fresh_o, fresh_ml,
    part, part_m, part_recv, part_m_recv, shared, shared_m, result,
    near_sem, in_sem, cache_sem, row_ssem, row_rsem, meta_sem,
    part_ssem, part_rsem, share_ssem, share_rsem, res_ssem, res_rsem,
):
    reqs, heads, kept, width = merged.shape
    pairs = reqs * heads
    evict = evict_v.shape[2]
    steps, _, _, depth = query_v.shape
    rows = query_s.shape[1]
    group = rows // steps
    slots = shards * cap
    scale = 1.0 / math.sqrt(depth)
    me = lax.axis_index("seq")
    core = lax.axis_index("hd")

    def peer(d):
        return lax.rem(me + d, shards)

    def source(d):
        return lax.rem(me + shards - d, shards)

    def remote(src, dst, ssem, rsem, device):
        return pltpu.make_async_remote_copy(
            src_ref=src, dst_ref=dst, send_sem=ssem, recv_sem=rsem,
            device_id={"seq": device}, device_id_type=pl.DeviceIdType.MESH,
        )

    def tell(sem, device):
        pl.semaphore_signal(
            sem, inc=1, device_id={"seq": device}, device_id_type=pl.DeviceIdType.MESH
        )

    chain = len(chunks) > 1
    barrier = pltpu.get_barrier_semaphore()
    if chain:
        for m in range(shards):
            @pl.when(me == m)
            def _():
                for t in [m - 1] * (m > 0) + list(range(m + 1, shards)):
                    tell(barrier, t)
    else:
        for d in range(1, shards):
            tell(barrier, peer(d))

    small = [
        pltpu.make_async_copy(src, dst, in_sem.at[i])
        for i, (src, dst) in enumerate((
            (target, target_v), (weight, weight_v), (evicted, evict_v),
            (queries, query_v), (fresh, fresh_v), (counts, counts_v),
        ))
    ]
    for copy in small:
        copy.start()
    load = pltpu.make_async_copy(cache, merged, cache_sem.at[0])
    load.start()

    ahead = lax.broadcasted_iota(jnp.int32, (rows, 128), 1) - lax.broadcasted_iota(
        jnp.int32, (rows, 128), 0
    )
    spot = {first + j: j * rows for first, count, _ in plan for j in range(count)}

    def to_row(*placed):
        grid = jnp.zeros((rows, 128), F32)
        for column, at in placed:
            grid = jnp.where(ahead == at, column, grid)
        return jnp.sum(grid, axis=0, keepdims=True)

    def to_column(row, at):
        return jnp.sum(jnp.where(ahead == at, row, 0.0), axis=1, keepdims=True)

    def attend_new():
        padded = -(-steps // 16) * 16
        new_step = lax.broadcasted_iota(jnp.int32, (rows, padded), 1)
        row_index = lax.broadcasted_iota(jnp.int32, (rows, padded), 0)
        allowed = row_index < 0
        for s in range(steps):
            allowed = allowed | ((new_step == s) & (row_index >= s * group))
        for r in range(reqs):
            asked = [query_v[s, r].astype(F32) for s in range(steps)]
            added = [fresh_v[s, r].astype(F32) for s in range(steps)]
            for h in range(heads):
                i = r * heads + h
                query = jnp.concatenate(
                    [a[h * group : (h + 1) * group] for a in asked], axis=0
                ).astype(BF16)
                query_s[i] = query
                latest = jnp.concatenate(
                    [a[h : h + 1] for a in added] + [jnp.zeros((padded - steps, width), F32)],
                    axis=0,
                ).astype(BF16)
                highest, total, weighted = softmax_block(
                    query, latest[:, :depth], latest[:, depth:], allowed, scale
                )
                fresh_o[i] = weighted
                fresh_ml[i, 0:1, :] = to_row((highest, spot[i]))
                fresh_ml[i, 1:2, :] = to_row((total, spot[i]))

    for copy in small[3:]:
        copy.wait()

    @pl.when(core != 0)
    def _():
        attend_new()

    for copy in small[:3]:
        copy.wait()
    aimed = jnp.concatenate([target_v[r] for r in range(reqs)], axis=0)
    weights = jnp.concatenate([weight_v[r].astype(F32) for r in range(reqs)], axis=0)
    owned, position, base = [], jnp.zeros_like(aimed), jnp.zeros(aimed.shape, F32)
    for d in range(shards):
        low = peer(d) * kept
        mine = (aimed >= low) & (aimed < low + kept)
        owned.append(jnp.where(mine, 1.0, 0.0))
        position = jnp.where(mine, aimed - low, position)
        base = jnp.where(mine, float(d * cap), base)
    above = lax.broadcasted_iota(jnp.int32, (evict, evict), 0) < lax.broadcasted_iota(
        jnp.int32, (evict, evict), 1
    )
    earlier = jnp.dot(
        jnp.concatenate(owned, axis=0).astype(BF16),
        jnp.where(above, 1.0, 0.0).astype(BF16),
        preferred_element_type=F32,
    )
    slot = base
    for d in range(shards):
        slot = slot + owned[d] * earlier[d * pairs : (d + 1) * pairs]
    slot = slot.astype(jnp.int32)
    features = jnp.concatenate(
        [weights, (position & 255).astype(F32), (position >> 8).astype(F32)], axis=0
    ).astype(BF16)
    slot_row = lax.broadcasted_iota(jnp.int32, (slots, evict), 0)

    def pack(i):
        r, h = divmod(i, heads)
        packing = jnp.where(slot_row == slot[i : i + 1, :], 1.0, 0.0).astype(BF16)
        packed = jnp.dot(packing, evict_v[r, h], preferred_element_type=F32).astype(BF16)
        send[i] = packed
        recv[i, 0:cap, :] = packed[0:cap]
        meta = contract_last(features, packing)
        meta_send[i : i + 1, :] = (
            (meta[2 * pairs + i : 2 * pairs + i + 1] * 256.0 + meta[pairs + i : pairs + i + 1])
            * 2048.0 + meta[i : i + 1] * 512.0
        )

    others = pl.ds(1, shards - 1)

    def all_of(ref, ssem, rsem):
        return remote(ref, ref, ssem, rsem, peer(1))

    def send_rows(c, d):
        first, count = chunks[c]
        lot = (pl.ds(first, count), pl.ds(d * cap, cap))
        remote(send.at[lot], recv.at[lot], row_ssem.at[0], row_rsem.at[c], peer(d)).start()

    def send_meta(d):
        remote(meta_send, meta_recv.at[d], meta_sem.at[0], meta_sem.at[1], peer(d)).start()

    def rows_in(c):
        first, count = chunks[c]
        lot = (pl.ds(first, count), pl.ds(cap, slots - cap))
        return all_of(recv.at[lot], row_ssem.at[0], row_rsem.at[c])

    def send_rest(m):
        there = sorted((t for t in range(shards) if t != m), key=lambda t: -abs(t - m))
        edge = m in (0, shards - 1)
        for c in range(1, len(chunks)):
            for t in there[:-1] if edge else there:
                send_rows(c, (t - m) % shards)
        if edge:
            for c in range(1, len(chunks)):
                send_rows(c, (there[-1] - m) % shards)

    for i in range(chunks[0][1]):
        pack(i)

    if chain:
        for m in range(shards):
            @pl.when(me == m)
            def _():
                pl.semaphore_wait(barrier, m + (m < shards - 1))
                if 0 < m < shards - 1:
                    tell(near_sem.at[0], m - 1)
                for t in range(m):
                    send_rows(0, (t - m) % shards)
                if m < shards - 1:
                    send_rows(0, 1)

    for i in range(chunks[0][1], pairs):
        pack(i)

    if chain:
        @pl.when(core == 0)
        def _():
            attend_new()

        for m in range(shards):
            @pl.when(me == m)
            def _():
                for far in range(2, shards - m):
                    pl.semaphore_wait(near_sem.at[far - 2], 1)
                    if m > 0:
                        tell(near_sem.at[far - 1], m - 1)
                    send_rows(0, far)
                there = sorted((t for t in range(shards) if t != m), key=lambda t: -abs(t - m))
                for t in there:
                    send_meta((t - m) % shards)

                @pl.when(core == 0)
                def _():
                    send_rest(m)
    else:
        pl.semaphore_wait(barrier, shards - 1)
        for d in range(1, shards):
            send_meta(d)
        for c in range(len(chunks)):
            for d in range(1, shards):
                send_rows(c, d)

        @pl.when(core == 0)
        def _():
            attend_new()

    meta_in = all_of(meta_recv.at[others], meta_sem.at[0], meta_sem.at[1])
    meta_in.wait_recv()
    lane = lax.broadcasted_iota(jnp.int32, (pairs, slots), 1)
    meta = meta_send[...]
    for d in range(1, shards):
        meta = jnp.where(lane >= d * cap, meta_recv[d], meta)
    slot_position = (meta * (1.0 / 2048.0)).astype(jnp.int32)
    slot_weight = (meta - slot_position.astype(F32) * 2048.0) * (1.0 / 512.0)

    kept_row = lax.broadcasted_iota(jnp.int32, (kept, slots), 0).astype(jnp.int16)
    kept_lane = lax.broadcasted_iota(jnp.int32, (rows, kept), 1)
    ones = jnp.ones((slots, 128), BF16)

    def merge(i):
        r, h = divmod(i, heads)
        aims = jnp.broadcast_to(slot_position[i : i + 1], (16, slots)).astype(jnp.int16)
        gains = jnp.broadcast_to(slot_weight[i : i + 1], (16, slots)).astype(BF16)
        placing = jnp.where(
            kept_row == jnp.concatenate([aims] * (kept // 16), axis=0),
            jnp.concatenate([gains] * (kept // 16), axis=0),
            jnp.zeros((kept, slots), BF16),
        )
        factor = 1.0 / (1.0 + jnp.dot(placing, ones, preferred_element_type=F32))
        if i == 0:
            load.wait()
        for c, (first, _) in enumerate(chunks):
            if first == i:
                rows_in(c).wait_recv()
        if chain and i == 0:
            for m in range(shards):
                @pl.when((me == m) & (core != 0))
                def _():
                    send_rest(m)
        summed = jnp.dot(placing, recv[i], preferred_element_type=F32)
        factor = jnp.concatenate([factor] * (width // 128), axis=1)
        fused = ((merged[r, h].astype(F32) + summed) * factor).astype(BF16)
        merged[r, h] = fused
        return softmax_block(
            query_s[i], fused[:, :depth], fused[:, depth:], kept_lane < counts_v[:, r : r + 1], scale
        )

    def to_owner(k, count, owner):
        lot = pl.ds(0, count * rows)
        away = lax.rem(owner - me + shards, shards)
        return (
            remote(
                part.at[k, lot], part_recv.at[0, away, lot],
                part_ssem.at[k, 0], part_rsem.at[0, 0], owner,
            ),
            remote(
                part_m.at[k], part_m_recv.at[0, away],
                part_ssem.at[k, 1], part_rsem.at[0, 1], owner,
            ),
        )

    def parts_in(k, count):
        lot = pl.ds(0, count * rows)
        return (
            all_of(part_recv.at[0, others, lot], part_ssem.at[k, 0], part_rsem.at[0, 0]),
            all_of(part_m_recv.at[0, others], part_ssem.at[k, 1], part_rsem.at[0, 1]),
        )

    def share_rows(k, j, d):
        lot = shared.at[k, me, pl.ds(j * rows, rows)]
        return remote(lot, lot, share_ssem.at[k, 0], share_rsem.at[k, 0], peer(d))

    def share_tops(k, d):
        lot = shared_m.at[k, me]
        return remote(lot, lot, share_ssem.at[k, 1], share_rsem.at[k, 1], peer(d))

    def shares(k, count):
        lot = pl.ds(0, count * rows)
        return (
            all_of(shared.at[k, others, lot], share_ssem.at[k, 0], share_rsem.at[k, 0]),
            all_of(shared_m.at[k, others], share_ssem.at[k, 1], share_rsem.at[k, 1]),
        )

    def send_result(k, first, count, d):
        lot = result.at[pl.ds(first, count)]
        return remote(lot, lot, res_ssem.at[0], res_rsem.at[k], peer(d))

    owned_plan = [(k, *entry) for k, entry in enumerate(plan) if entry[2] is not None]
    owned_index = {entry[0]: n for n, entry in enumerate(owned_plan)}
    shared_plan = [(k, *entry) for k, entry in enumerate(plan) if entry[2] is None]
    shared_index = {entry[0]: n for n, entry in enumerate(shared_plan)}

    for k, (first, count, owner) in enumerate(plan):
        tops, sums = [], []
        for j in range(count):
            highest, total, weighted = merge(first + j)
            size = jnp.maximum(jnp.max(jnp.abs(weighted), axis=-1, keepdims=True), 1e-30)
            coded = jnp.round(weighted * (32767.0 / size)).astype(jnp.int32).astype(jnp.int16)
            if owner is None:
                into, into_m = shared.at[shared_index[k], me], shared_m.at[shared_index[k], me]
            else:
                into, into_m = part.at[owned_index[k]], part_m.at[owned_index[k]]
            into[j * rows : (j + 1) * rows, :] = coded
            if owner is None:
                for d in range(1, shards):
                    share_rows(shared_index[k], j, d).start()
            at = j * rows
            tops.append(to_row((highest, at), (size * (1.0 / 32767.0), at + 64)))
            sums.append(to_row((total, at)))
        into_m[0:1, :] = functools.reduce(jnp.add, tops)
        into_m[1:2, :] = functools.reduce(jnp.add, sums)
        if owner is None:
            for d in range(1, shards):
                share_tops(shared_index[k], d).start()
        else:
            @pl.when(me != owner)
            def _():
                for copy in to_owner(owned_index[k], count, owner):
                    copy.start()

    lanes = lax.broadcasted_iota(jnp.int32, (1, 128), 1)

    def combine(first, count, blocks):
        group = range(first, first + count)
        tiles = [
            (
                functools.reduce(jnp.add, [fresh_ml[i, 0:1, :] for i in group]),
                functools.reduce(jnp.add, [fresh_ml[i, 1:2, :] for i in group]),
            )
        ] + [(m[0:1, :], m[1:2, :]) for _, m in blocks]
        top = functools.reduce(jnp.maximum, [tile[0] for tile in tiles])
        shares = [jnp.exp(tile[0] - top) for tile in tiles]
        total = functools.reduce(jnp.add, [a * tile[1] for a, tile in zip(shares, tiles)])
        shares = [a / jnp.where(lanes < count * rows, total, 1.0) for a in shares]
        for n, (_, m) in enumerate(blocks):
            scales = jnp.concatenate([m[0:1, 64:], m[0:1, :64]], axis=1)
            shares[n + 1] = shares[n + 1] * scales
        for j, i in enumerate(group):
            blend = to_column(shares[0], j * rows) * fresh_o[i]
            for share, (b, _) in zip(shares[1:], blocks):
                out = b[j * rows : (j + 1) * rows, :].astype(jnp.int32).astype(F32)
                blend = blend + to_column(share, j * rows) * out
            result[i] = blend.astype(BF16)

    for k, first, count, owner in owned_plan:
        n = owned_index[k]

        @pl.when(me == owner)
        def _():
            for copy in parts_in(n, count):
                copy.wait_recv()
            combine(
                first, count,
                [(part.at[n], part_m.at[n])]
                + [(part_recv.at[0, d], part_m_recv.at[0, d]) for d in range(1, shards)],
            )
            for d in range(1, shards):
                send_result(n, first, count, d).start()

    for k, first, count, _ in shared_plan:
        n = shared_index[k]
        for copy in shares(n, count):
            copy.wait_recv()
        combine(first, count, [(shared.at[n, d], shared_m.at[n, d]) for d in range(shards)])

    for k, first, count, owner in owned_plan:
        @pl.when(me != owner)
        def _():
            send_result(owned_index[k], first, count, 1).wait_recv()

    for r in range(reqs):
        done = [result[r * heads + h].astype(F32) for h in range(heads)]
        for s in range(steps):
            attended[s, r] = jnp.concatenate(
                [a[s * group : (s + 1) * group] for a in done], axis=0
            ).astype(BF16)

    meta_in.wait_send()
    sent = (pl.ds(0, pairs), pl.ds(cap, slots - cap))
    all_of(recv.at[sent], row_ssem.at[0], row_rsem.at[0]).wait_send()
    for k, first, count, owner in owned_plan:
        n = owned_index[k]

        @pl.when(me != owner)
        def _():
            for copy in to_owner(n, count, owner):
                copy.wait_send()

        @pl.when(me == owner)
        def _():
            lot = part_recv.at[0, others, pl.ds(0, count * rows)]
            all_of(lot, res_ssem.at[0], res_rsem.at[n]).wait_send()

    for k, first, count, _ in shared_plan:
        for copy in shares(shared_index[k], count):
            copy.wait_send()


def write_out(merged, attended, merged_out, attended_out, sem):
    copies = [
        pltpu.make_async_copy(merged, merged_out, sem.at[0]),
        pltpu.make_async_copy(attended, attended_out, sem.at[1]),
    ]
    for copy in copies:
        copy.start()
    for copy in copies:
        copy.wait()


def schedule(shards, pairs):
    per = max(1, min(2, pairs // shards))
    firsts = list(range(0, pairs, per))
    near = shards <= 8
    late = len(firsts) // 2 if near else 0
    plan = []
    for n, first in enumerate(firsts):
        owner = (shards // 2 - 1 + n) % shards if near else n % shards
        plan.append((first, min(per, pairs - first), owner if n < len(firsts) - late else None))
    return tuple(plan)


def row_chunks(shards, pairs):
    if shards > 8 or shards < 3:
        return ((0, pairs),)
    head = max(1, 3 * pairs // 8)
    return ((0, head),) + tuple((i, 1) for i in range(head, pairs))


def body(shards, cache, evicted, merge_weight, targets, kept_counts, queries, new_rows):
    reqs, heads, kept, width = cache.shape
    pairs = reqs * heads
    evict = evicted.shape[2]
    steps, _, query_local, depth = queries.shape
    rows = steps * query_local // heads
    cap = -(-max(2, 2 * evict // shards) // 16) * 16
    slots = shards * cap
    chunks = row_chunks(shards, pairs)
    plan = schedule(shards, pairs)
    most = max(count for _, count, _ in plan)
    owned = max(1, sum(owner is not None for _, _, owner in plan))
    common = max(1, len(plan) - owned)
    assert most * rows <= 64
    high = 2
    dma = pltpu.SemaphoreType.DMA
    done = pl.pallas_call(
        functools.partial(kernel, shards, cap, chunks, plan),
        out_shape=(
            jax.ShapeDtypeStruct(cache.shape, BF16),
            jax.ShapeDtypeStruct(queries.shape, BF16),
        ),
        in_specs=[pl.BlockSpec(memory_space=pltpu.HBM)] * 7,
        out_specs=(pl.BlockSpec(memory_space=pltpu.VMEM),) * 2,
        scratch_shapes=[
            pltpu.VMEM(evicted.shape, BF16),
            pltpu.VMEM(merge_weight.shape, BF16),
            pltpu.VMEM(targets.shape, jnp.int32),
            pltpu.VMEM(kept_counts.shape[::-1], jnp.int32),
            pltpu.VMEM(queries.shape, BF16),
            pltpu.VMEM(new_rows.shape, BF16),
            pltpu.VMEM((pairs, slots, width), BF16),
            pltpu.VMEM((pairs, slots, width), BF16),
            pltpu.VMEM((pairs, slots), F32),
            pltpu.VMEM((shards, pairs, slots), F32),
            pltpu.VMEM((pairs, rows, depth), BF16),
            pltpu.VMEM((pairs, rows, depth), F32),
            pltpu.VMEM((pairs, 2, 128), F32),
            pltpu.VMEM((owned, most * rows, depth), jnp.int16),
            pltpu.VMEM((owned, high, 128), F32),
            pltpu.VMEM((1, shards, most * rows, depth), jnp.int16),
            pltpu.VMEM((1, shards, high, 128), F32),
            pltpu.VMEM((common, shards, most * rows, depth), jnp.int16),
            pltpu.VMEM((common, shards, high, 128), F32),
            pltpu.VMEM((pairs, rows, depth), BF16),
            pltpu.SemaphoreType.REGULAR((max(1, shards - 2),)),
            dma((6,)),
            dma((1,)),
            dma((1,)),
            dma((len(chunks),)),
            dma((2,)),
            dma((owned, 2)),
            dma((1, 2)),
            dma((common, 2)),
            dma((common, 2)),
            dma((1,)),
            dma((owned,)),
        ],
        compiler_params=pltpu.CompilerParams(
            collective_id=0, has_side_effects=True, vmem_limit_bytes=48 * 1024 * 1024
        ),
    )(*(
        pltpu.with_memory_space_constraint(a, pltpu.HBM)
        for a in (cache, evicted, merge_weight, targets, kept_counts.T, queries, new_rows)
    ))
    return pl.pallas_call(
        write_out,
        out_shape=tuple(jax.ShapeDtypeStruct(a.shape, a.dtype) for a in done),
        in_specs=[pl.BlockSpec(memory_space=pltpu.VMEM)] * 2,
        out_specs=(pl.BlockSpec(memory_space=pltpu.HBM),) * 2,
        scratch_shapes=[dma((2,))],
    )(*(pltpu.with_memory_space_constraint(a, pltpu.VMEM) for a in done))


def solution(mesh):
    return jax.shard_map(
        functools.partial(body, mesh.shape["seq"]),
        mesh=mesh,
        in_specs=(
            P(("grp", "req"), "hd", "seq", None),
            P(("grp", "req"), "hd", "seq", None),
            P(("grp", "req"), "hd", "seq"),
            P(("grp", "req"), "hd", "seq"),
            P(("grp", "req"), "seq"),
            P(None, ("grp", "req"), "hd", None),
            P(None, ("grp", "req"), "hd", None),
        ),
        out_specs=(P(("grp", "req"), "hd", "seq", None), P(None, ("grp", "req"), "hd", None)),
        check_vma=False,
    )
```

```python
import functools
import math

import jax
import jax.numpy as jnp
from jax import lax
from jax.experimental import pallas as pl
from jax.experimental.pallas import tpu as pltpu
from jax.sharding import PartitionSpec as P

F32 = jnp.float32
BF16 = jnp.bfloat16
NEG = -1e30


def contract_last(a, b):
    return lax.dot_general(a, b, (((1,), (1,)), ((), ())), preferred_element_type=F32)


def softmax_block(query, keys, values, allowed, scale):
    scores = jnp.where(allowed, contract_last(query, keys) * scale, NEG)
    highest = jnp.max(scores, axis=-1, keepdims=True)
    exponent = jnp.exp(scores - highest)
    total = jnp.sum(exponent, axis=-1, keepdims=True)
    weighted = jnp.dot(exponent.astype(BF16), values, preferred_element_type=F32)
    return highest, total, weighted


def kernel(
    shards, cap, chunks, plan,
    cache, evicted, weight, target, counts, queries, fresh,
    merged, attended,
    evict_v, weight_v, target_v, counts_v, query_v, fresh_v,
    send, recv, meta_send, meta_recv, query_s, fresh_o, fresh_ml,
    part, part_m, part_recv, part_m_recv, shared, shared_m, result,
    near_sem, in_sem, cache_sem, row_ssem, row_rsem, meta_sem,
    part_ssem, part_rsem, share_ssem, share_rsem, res_ssem, res_rsem,
):
    reqs, heads, kept, width = merged.shape
    pairs = reqs * heads
    evict = evict_v.shape[2]
    steps, _, _, depth = query_v.shape
    rows = query_s.shape[1]
    group = rows // steps
    slots = shards * cap
    scale = 1.0 / math.sqrt(depth)
    me = lax.axis_index("seq")
    core = lax.axis_index("hd")

    def peer(d):
        return lax.rem(me + d, shards)

    def source(d):
        return lax.rem(me + shards - d, shards)

    def remote(src, dst, ssem, rsem, device):
        return pltpu.make_async_remote_copy(
            src_ref=src, dst_ref=dst, send_sem=ssem, recv_sem=rsem,
            device_id={"seq": device}, device_id_type=pl.DeviceIdType.MESH,
        )

    def tell(sem, device):
        pl.semaphore_signal(
            sem, inc=1, device_id={"seq": device}, device_id_type=pl.DeviceIdType.MESH
        )

    chain = len(chunks) > 1
    barrier = pltpu.get_barrier_semaphore()
    if chain:
        for m in range(shards):
            @pl.when(me == m)
            def _():
                for t in [m - 1] * (m > 0) + list(range(m + 1, shards)):
                    tell(barrier, t)
    else:
        for d in range(1, shards):
            tell(barrier, peer(d))

    small = [
        pltpu.make_async_copy(src, dst, in_sem.at[i])
        for i, (src, dst) in enumerate((
            (target, target_v), (weight, weight_v), (evicted, evict_v),
            (queries, query_v), (fresh, fresh_v), (counts, counts_v),
        ))
    ]
    for copy in small:
        copy.start()
    load = pltpu.make_async_copy(cache, merged, cache_sem.at[0])
    load.start()

    ahead = lax.broadcasted_iota(jnp.int32, (rows, 128), 1) - lax.broadcasted_iota(
        jnp.int32, (rows, 128), 0
    )
    spot = {first + j: j * rows for first, count, _ in plan for j in range(count)}

    def to_row(*placed):
        grid = jnp.zeros((rows, 128), F32)
        for column, at in placed:
            grid = jnp.where(ahead == at, column, grid)
        return jnp.sum(grid, axis=0, keepdims=True)

    def to_column(row, at):
        return jnp.sum(jnp.where(ahead == at, row, 0.0), axis=1, keepdims=True)

    def attend_new():
        padded = -(-steps // 16) * 16
        new_step = lax.broadcasted_iota(jnp.int32, (rows, padded), 1)
        row_index = lax.broadcasted_iota(jnp.int32, (rows, padded), 0)
        allowed = row_index < 0
        for s in range(steps):
            allowed = allowed | ((new_step == s) & (row_index >= s * group))
        for r in range(reqs):
            asked = [query_v[s, r].astype(F32) for s in range(steps)]
            added = [fresh_v[s, r].astype(F32) for s in range(steps)]
            for h in range(heads):
                i = r * heads + h
                query = jnp.concatenate(
                    [a[h * group : (h + 1) * group] for a in asked], axis=0
                ).astype(BF16)
                query_s[i] = query
                latest = jnp.concatenate(
                    [a[h : h + 1] for a in added] + [jnp.zeros((padded - steps, width), F32)],
                    axis=0,
                ).astype(BF16)
                highest, total, weighted = softmax_block(
                    query, latest[:, :depth], latest[:, depth:], allowed, scale
                )
                fresh_o[i] = weighted
                fresh_ml[i, 0:1, :] = to_row((highest, spot[i]))
                fresh_ml[i, 1:2, :] = to_row((total, spot[i]))

    for copy in small[3:]:
        copy.wait()

    @pl.when(core != 0)
    def _():
        attend_new()

    for copy in small[:3]:
        copy.wait()
    aimed = jnp.concatenate([target_v[r] for r in range(reqs)], axis=0)
    weights = jnp.concatenate([weight_v[r].astype(F32) for r in range(reqs)], axis=0)
    owned, position, base = [], jnp.zeros_like(aimed), jnp.zeros(aimed.shape, F32)
    for d in range(shards):
        low = peer(d) * kept
        mine = (aimed >= low) & (aimed < low + kept)
        owned.append(jnp.where(mine, 1.0, 0.0))
        position = jnp.where(mine, aimed - low, position)
        base = jnp.where(mine, float(d * cap), base)
    above = lax.broadcasted_iota(jnp.int32, (evict, evict), 0) < lax.broadcasted_iota(
        jnp.int32, (evict, evict), 1
    )
    earlier = jnp.dot(
        jnp.concatenate(owned, axis=0).astype(BF16),
        jnp.where(above, 1.0, 0.0).astype(BF16),
        preferred_element_type=F32,
    )
    slot = base
    for d in range(shards):
        slot = slot + owned[d] * earlier[d * pairs : (d + 1) * pairs]
    slot = slot.astype(jnp.int32)
    features = jnp.concatenate(
        [weights, (position & 255).astype(F32), (position >> 8).astype(F32)], axis=0
    ).astype(BF16)
    slot_row = lax.broadcasted_iota(jnp.int32, (slots, evict), 0)

    def pack(i):
        r, h = divmod(i, heads)
        packing = jnp.where(slot_row == slot[i : i + 1, :], 1.0, 0.0).astype(BF16)
        packed = jnp.dot(packing, evict_v[r, h], preferred_element_type=F32).astype(BF16)
        send[i] = packed
        recv[i, 0:cap, :] = packed[0:cap]
        meta = contract_last(features, packing)
        meta_send[i : i + 1, :] = (
            (meta[2 * pairs + i : 2 * pairs + i + 1] * 256.0 + meta[pairs + i : pairs + i + 1])
            * 2048.0 + meta[i : i + 1] * 512.0
        )

    others = pl.ds(1, shards - 1)

    def all_of(ref, ssem, rsem):
        return remote(ref, ref, ssem, rsem, peer(1))

    def send_rows(c, d):
        first, count = chunks[c]
        lot = (pl.ds(first, count), pl.ds(d * cap, cap))
        remote(send.at[lot], recv.at[lot], row_ssem.at[0], row_rsem.at[c], peer(d)).start()

    def send_meta(d):
        remote(meta_send, meta_recv.at[d], meta_sem.at[0], meta_sem.at[1], peer(d)).start()

    def rows_in(c):
        first, count = chunks[c]
        lot = (pl.ds(first, count), pl.ds(cap, slots - cap))
        return all_of(recv.at[lot], row_ssem.at[0], row_rsem.at[c])

    def send_rest(m, low, high):
        there = sorted((t for t in range(shards) if t != m), key=lambda t: -abs(t - m))
        edge = m in (0, shards - 1)
        for c in range(low, high):
            for t in there[:-1] if edge else there:
                send_rows(c, (t - m) % shards)
        if edge:
            for c in range(low, high):
                send_rows(c, (there[-1] - m) % shards)

    for i in range(chunks[0][1]):
        pack(i)

    if chain:
        for m in range(shards):
            @pl.when(me == m)
            def _():
                pl.semaphore_wait(barrier, m + (m < shards - 1))
                if 0 < m < shards - 1:
                    tell(near_sem.at[0], m - 1)
                for t in range(m):
                    send_rows(0, (t - m) % shards)
                if m < shards - 1:
                    send_rows(0, 1)

    for i in range(chunks[0][1], pairs):
        pack(i)

    if chain:
        @pl.when(core == 0)
        def _():
            attend_new()

        for m in range(shards):
            @pl.when(me == m)
            def _():
                for far in range(2, shards - m):
                    pl.semaphore_wait(near_sem.at[far - 2], 1)
                    if m > 0:
                        tell(near_sem.at[far - 1], m - 1)
                    send_rows(0, far)
                there = sorted((t for t in range(shards) if t != m), key=lambda t: -abs(t - m))
                for t in there:
                    send_meta((t - m) % shards)

                keep = 0 if 0 < m < shards - 1 else 1

                @pl.when(core == 0)
                def _():
                    send_rest(m, 1, len(chunks) - keep)
    else:
        pl.semaphore_wait(barrier, shards - 1)
        for d in range(1, shards):
            send_meta(d)
        for c in range(len(chunks)):
            for d in range(1, shards):
                send_rows(c, d)

        @pl.when(core == 0)
        def _():
            attend_new()

    meta_in = all_of(meta_recv.at[others], meta_sem.at[0], meta_sem.at[1])
    meta_in.wait_recv()
    lane = lax.broadcasted_iota(jnp.int32, (pairs, slots), 1)
    meta = meta_send[...]
    for d in range(1, shards):
        meta = jnp.where(lane >= d * cap, meta_recv[d], meta)
    slot_position = (meta * (1.0 / 2048.0)).astype(jnp.int32)
    slot_weight = (meta - slot_position.astype(F32) * 2048.0) * (1.0 / 512.0)

    kept_row = lax.broadcasted_iota(jnp.int32, (kept, slots), 0).astype(jnp.int16)
    kept_lane = lax.broadcasted_iota(jnp.int32, (rows, kept), 1)
    ones = jnp.ones((slots, 128), BF16)

    def merge(i):
        r, h = divmod(i, heads)
        aims = jnp.broadcast_to(slot_position[i : i + 1], (16, slots)).astype(jnp.int16)
        gains = jnp.broadcast_to(slot_weight[i : i + 1], (16, slots)).astype(BF16)
        placing = jnp.where(
            kept_row == jnp.concatenate([aims] * (kept // 16), axis=0),
            jnp.concatenate([gains] * (kept // 16), axis=0),
            jnp.zeros((kept, slots), BF16),
        )
        factor = 1.0 / (1.0 + jnp.dot(placing, ones, preferred_element_type=F32))
        if i == 0:
            load.wait()
        for c, (first, _) in enumerate(chunks):
            if first == i:
                rows_in(c).wait_recv()
        if chain and i == 0:
            for m in range(shards):
                @pl.when((me == m) & (core != 0))
                def _():
                    send_rest(m, 1, len(chunks))

                keep = 0 if 0 < m < shards - 1 else 1
                if keep:
                    @pl.when((me == m) & (core == 0))
                    def _():
                        send_rest(m, len(chunks) - keep, len(chunks))
        summed = jnp.dot(placing, recv[i], preferred_element_type=F32)
        factor = jnp.concatenate([factor] * (width // 128), axis=1)
        fused = ((merged[r, h].astype(F32) + summed) * factor).astype(BF16)
        merged[r, h] = fused
        return softmax_block(
            query_s[i], fused[:, :depth], fused[:, depth:], kept_lane < counts_v[:, r : r + 1], scale
        )

    def to_owner(k, count, owner):
        lot = pl.ds(0, count * rows)
        away = lax.rem(owner - me + shards, shards)
        return (
            remote(
                part.at[k, lot], part_recv.at[0, away, lot],
                part_ssem.at[k, 0], part_rsem.at[0, 0], owner,
            ),
            remote(
                part_m.at[k], part_m_recv.at[0, away],
                part_ssem.at[k, 1], part_rsem.at[0, 1], owner,
            ),
        )

    def parts_in(k, count):
        lot = pl.ds(0, count * rows)
        return (
            all_of(part_recv.at[0, others, lot], part_ssem.at[k, 0], part_rsem.at[0, 0]),
            all_of(part_m_recv.at[0, others], part_ssem.at[k, 1], part_rsem.at[0, 1]),
        )

    def share_rows(k, j, d):
        lot = shared.at[k, me, pl.ds(j * rows, rows)]
        return remote(lot, lot, share_ssem.at[k, 0], share_rsem.at[k, 0], peer(d))

    def share_tops(k, d):
        lot = shared_m.at[k, me]
        return remote(lot, lot, share_ssem.at[k, 1], share_rsem.at[k, 1], peer(d))

    def shares(k, count):
        lot = pl.ds(0, count * rows)
        return (
            all_of(shared.at[k, others, lot], share_ssem.at[k, 0], share_rsem.at[k, 0]),
            all_of(shared_m.at[k, others], share_ssem.at[k, 1], share_rsem.at[k, 1]),
        )

    def send_result(k, first, count, d):
        lot = result.at[pl.ds(first, count)]
        return remote(lot, lot, res_ssem.at[0], res_rsem.at[k], peer(d))

    owned_plan = [(k, *entry) for k, entry in enumerate(plan) if entry[2] is not None]
    owned_index = {entry[0]: n for n, entry in enumerate(owned_plan)}
    shared_plan = [(k, *entry) for k, entry in enumerate(plan) if entry[2] is None]
    shared_index = {entry[0]: n for n, entry in enumerate(shared_plan)}

    for k, (first, count, owner) in enumerate(plan):
        tops, sums = [], []
        for j in range(count):
            highest, total, weighted = merge(first + j)
            size = jnp.maximum(jnp.max(jnp.abs(weighted), axis=-1, keepdims=True), 1e-30)
            coded = jnp.round(weighted * (32767.0 / size)).astype(jnp.int32).astype(jnp.int16)
            if owner is None:
                into, into_m = shared.at[shared_index[k], me], shared_m.at[shared_index[k], me]
            else:
                into, into_m = part.at[owned_index[k]], part_m.at[owned_index[k]]
            into[j * rows : (j + 1) * rows, :] = coded
            if owner is None:
                for d in range(1, shards):
                    share_rows(shared_index[k], j, d).start()
            at = j * rows
            tops.append(to_row((highest, at), (size * (1.0 / 32767.0), at + 64)))
            sums.append(to_row((total, at)))
        into_m[0:1, :] = functools.reduce(jnp.add, tops)
        into_m[1:2, :] = functools.reduce(jnp.add, sums)
        if owner is None:
            for d in range(1, shards):
                share_tops(shared_index[k], d).start()
        else:
            @pl.when(me != owner)
            def _():
                for copy in to_owner(owned_index[k], count, owner):
                    copy.start()

    lanes = lax.broadcasted_iota(jnp.int32, (1, 128), 1)

    def combine(first, count, blocks):
        group = range(first, first + count)
        tiles = [
            (
                functools.reduce(jnp.add, [fresh_ml[i, 0:1, :] for i in group]),
                functools.reduce(jnp.add, [fresh_ml[i, 1:2, :] for i in group]),
            )
        ] + [(m[0:1, :], m[1:2, :]) for _, m in blocks]
        top = functools.reduce(jnp.maximum, [tile[0] for tile in tiles])
        shares = [jnp.exp(tile[0] - top) for tile in tiles]
        total = functools.reduce(jnp.add, [a * tile[1] for a, tile in zip(shares, tiles)])
        shares = [a / jnp.where(lanes < count * rows, total, 1.0) for a in shares]
        for n, (_, m) in enumerate(blocks):
            scales = jnp.concatenate([m[0:1, 64:], m[0:1, :64]], axis=1)
            shares[n + 1] = shares[n + 1] * scales
        for j, i in enumerate(group):
            blend = to_column(shares[0], j * rows) * fresh_o[i]
            for share, (b, _) in zip(shares[1:], blocks):
                out = b[j * rows : (j + 1) * rows, :].astype(jnp.int32).astype(F32)
                blend = blend + to_column(share, j * rows) * out
            result[i] = blend.astype(BF16)

    for k, first, count, owner in owned_plan:
        n = owned_index[k]

        @pl.when(me == owner)
        def _():
            for copy in parts_in(n, count):
                copy.wait_recv()
            combine(
                first, count,
                [(part.at[n], part_m.at[n])]
                + [(part_recv.at[0, d], part_m_recv.at[0, d]) for d in range(1, shards)],
            )
            for d in range(1, shards):
                send_result(n, first, count, d).start()

    for k, first, count, _ in shared_plan:
        n = shared_index[k]
        for copy in shares(n, count):
            copy.wait_recv()
        combine(first, count, [(shared.at[n, d], shared_m.at[n, d]) for d in range(shards)])

    for k, first, count, owner in owned_plan:
        @pl.when(me != owner)
        def _():
            send_result(owned_index[k], first, count, 1).wait_recv()

    for r in range(reqs):
        done = [result[r * heads + h].astype(F32) for h in range(heads)]
        for s in range(steps):
            attended[s, r] = jnp.concatenate(
                [a[s * group : (s + 1) * group] for a in done], axis=0
            ).astype(BF16)

    meta_in.wait_send()
    sent = (pl.ds(0, pairs), pl.ds(cap, slots - cap))
    all_of(recv.at[sent], row_ssem.at[0], row_rsem.at[0]).wait_send()
    for k, first, count, owner in owned_plan:
        n = owned_index[k]

        @pl.when(me != owner)
        def _():
            for copy in to_owner(n, count, owner):
                copy.wait_send()

        @pl.when(me == owner)
        def _():
            lot = part_recv.at[0, others, pl.ds(0, count * rows)]
            all_of(lot, res_ssem.at[0], res_rsem.at[n]).wait_send()

    for k, first, count, _ in shared_plan:
        for copy in shares(shared_index[k], count):
            copy.wait_send()


def write_out(merged, attended, merged_out, attended_out, sem):
    copies = [
        pltpu.make_async_copy(merged, merged_out, sem.at[0]),
        pltpu.make_async_copy(attended, attended_out, sem.at[1]),
    ]
    for copy in copies:
        copy.start()
    for copy in copies:
        copy.wait()


def schedule(shards, pairs):
    per = max(1, min(2, pairs // shards))
    firsts = list(range(0, pairs, per))
    near = shards <= 8
    late = len(firsts) // 2 if near else 0
    plan = []
    for n, first in enumerate(firsts):
        owner = (shards // 2 - 1 + n) % shards if near else n % shards
        plan.append((first, min(per, pairs - first), owner if n < len(firsts) - late else None))
    return tuple(plan)


def row_chunks(shards, pairs):
    if shards > 8 or shards < 3:
        return ((0, pairs),)
    head = max(1, 3 * pairs // 8)
    return ((0, head),) + tuple((i, 1) for i in range(head, pairs))


def body(shards, cache, evicted, merge_weight, targets, kept_counts, queries, new_rows):
    reqs, heads, kept, width = cache.shape
    pairs = reqs * heads
    evict = evicted.shape[2]
    steps, _, query_local, depth = queries.shape
    rows = steps * query_local // heads
    cap = -(-max(2, 2 * evict // shards) // 16) * 16
    slots = shards * cap
    chunks = row_chunks(shards, pairs)
    plan = schedule(shards, pairs)
    most = max(count for _, count, _ in plan)
    owned = max(1, sum(owner is not None for _, _, owner in plan))
    common = max(1, len(plan) - owned)
    assert most * rows <= 64
    high = 2
    dma = pltpu.SemaphoreType.DMA
    done = pl.pallas_call(
        functools.partial(kernel, shards, cap, chunks, plan),
        out_shape=(
            jax.ShapeDtypeStruct(cache.shape, BF16),
            jax.ShapeDtypeStruct(queries.shape, BF16),
        ),
        in_specs=[pl.BlockSpec(memory_space=pltpu.HBM)] * 7,
        out_specs=(pl.BlockSpec(memory_space=pltpu.VMEM),) * 2,
        scratch_shapes=[
            pltpu.VMEM(evicted.shape, BF16),
            pltpu.VMEM(merge_weight.shape, BF16),
            pltpu.VMEM(targets.shape, jnp.int32),
            pltpu.VMEM(kept_counts.shape[::-1], jnp.int32),
            pltpu.VMEM(queries.shape, BF16),
            pltpu.VMEM(new_rows.shape, BF16),
            pltpu.VMEM((pairs, slots, width), BF16),
            pltpu.VMEM((pairs, slots, width), BF16),
            pltpu.VMEM((pairs, slots), F32),
            pltpu.VMEM((shards, pairs, slots), F32),
            pltpu.VMEM((pairs, rows, depth), BF16),
            pltpu.VMEM((pairs, rows, depth), F32),
            pltpu.VMEM((pairs, 2, 128), F32),
            pltpu.VMEM((owned, most * rows, depth), jnp.int16),
            pltpu.VMEM((owned, high, 128), F32),
            pltpu.VMEM((1, shards, most * rows, depth), jnp.int16),
            pltpu.VMEM((1, shards, high, 128), F32),
            pltpu.VMEM((common, shards, most * rows, depth), jnp.int16),
            pltpu.VMEM((common, shards, high, 128), F32),
            pltpu.VMEM((pairs, rows, depth), BF16),
            pltpu.SemaphoreType.REGULAR((max(1, shards - 2),)),
            dma((6,)),
            dma((1,)),
            dma((1,)),
            dma((len(chunks),)),
            dma((2,)),
            dma((owned, 2)),
            dma((1, 2)),
            dma((common, 2)),
            dma((common, 2)),
            dma((1,)),
            dma((owned,)),
        ],
        compiler_params=pltpu.CompilerParams(
            collective_id=0, has_side_effects=True, vmem_limit_bytes=48 * 1024 * 1024
        ),
    )(*(
        pltpu.with_memory_space_constraint(a, pltpu.HBM)
        for a in (cache, evicted, merge_weight, targets, kept_counts.T, queries, new_rows)
    ))
    return pl.pallas_call(
        write_out,
        out_shape=tuple(jax.ShapeDtypeStruct(a.shape, a.dtype) for a in done),
        in_specs=[pl.BlockSpec(memory_space=pltpu.VMEM)] * 2,
        out_specs=(pl.BlockSpec(memory_space=pltpu.HBM),) * 2,
        scratch_shapes=[dma((2,))],
    )(*(pltpu.with_memory_space_constraint(a, pltpu.VMEM) for a in done))


def solution(mesh):
    return jax.shard_map(
        functools.partial(body, mesh.shape["seq"]),
        mesh=mesh,
        in_specs=(
            P(("grp", "req"), "hd", "seq", None),
            P(("grp", "req"), "hd", "seq", None),
            P(("grp", "req"), "hd", "seq"),
            P(("grp", "req"), "hd", "seq"),
            P(("grp", "req"), "seq"),
            P(None, ("grp", "req"), "hd", None),
            P(None, ("grp", "req"), "hd", None),
        ),
        out_specs=(P(("grp", "req"), "hd", "seq", None), P(None, ("grp", "req"), "hd", None)),
        check_vma=False,
    )
```

```python
import functools
import math

import jax
import jax.numpy as jnp
from jax import lax
from jax.experimental import pallas as pl
from jax.experimental.pallas import tpu as pltpu
from jax.sharding import PartitionSpec as P

F32 = jnp.float32
BF16 = jnp.bfloat16
NEG = -1e30


def contract_last(a, b):
    return lax.dot_general(a, b, (((1,), (1,)), ((), ())), preferred_element_type=F32)


def softmax_block(query, keys, values, allowed, scale):
    scores = jnp.where(allowed, contract_last(query, keys) * scale, NEG)
    highest = jnp.max(scores, axis=-1, keepdims=True)
    exponent = jnp.exp(scores - highest)
    total = jnp.sum(exponent, axis=-1, keepdims=True)
    weighted = jnp.dot(exponent.astype(BF16), values, preferred_element_type=F32)
    return highest, total, weighted


def kernel(
    shards, cap, chunks, plan,
    cache, evicted, weight, target, counts, queries, fresh,
    merged, attended,
    evict_v, weight_v, target_v, counts_v, query_v, fresh_v,
    send, recv, meta_send, meta_recv, query_s, fresh_o, fresh_ml,
    part, part_m, part_recv, part_m_recv, shared, shared_m, result,
    near_sem, in_sem, cache_sem, row_ssem, row_rsem, meta_sem,
    part_ssem, part_rsem, share_ssem, share_rsem, res_ssem, res_rsem,
):
    reqs, heads, kept, width = merged.shape
    pairs = reqs * heads
    evict = evict_v.shape[2]
    steps, _, _, depth = query_v.shape
    rows = query_s.shape[1]
    group = rows // steps
    slots = shards * cap
    scale = 1.0 / math.sqrt(depth)
    me = lax.axis_index("seq")
    core = lax.axis_index("hd")

    def peer(d):
        return lax.rem(me + d, shards)

    def source(d):
        return lax.rem(me + shards - d, shards)

    def remote(src, dst, ssem, rsem, device):
        return pltpu.make_async_remote_copy(
            src_ref=src, dst_ref=dst, send_sem=ssem, recv_sem=rsem,
            device_id={"seq": device}, device_id_type=pl.DeviceIdType.MESH,
        )

    def tell(sem, device):
        pl.semaphore_signal(
            sem, inc=1, device_id={"seq": device}, device_id_type=pl.DeviceIdType.MESH
        )

    chain = len(chunks) > 1
    barrier = pltpu.get_barrier_semaphore()
    if chain:
        for m in range(shards):
            @pl.when(me == m)
            def _():
                for t in [m - 1] * (m > 0) + list(range(m + 1, shards)):
                    tell(barrier, t)
    else:
        for d in range(1, shards):
            tell(barrier, peer(d))

    small = [
        pltpu.make_async_copy(src, dst, in_sem.at[i])
        for i, (src, dst) in enumerate((
            (target, target_v), (weight, weight_v), (evicted, evict_v),
            (queries, query_v), (fresh, fresh_v), (counts, counts_v),
        ))
    ]
    for copy in small:
        copy.start()
    load = pltpu.make_async_copy(cache, merged, cache_sem.at[0])
    load.start()

    ahead = lax.broadcasted_iota(jnp.int32, (rows, 128), 1) - lax.broadcasted_iota(
        jnp.int32, (rows, 128), 0
    )
    spot = {first + j: j * rows for first, count, _ in plan for j in range(count)}

    def to_row(*placed):
        grid = jnp.zeros((rows, 128), F32)
        for column, at in placed:
            grid = jnp.where(ahead == at, column, grid)
        return jnp.sum(grid, axis=0, keepdims=True)

    def to_column(row, at):
        return jnp.sum(jnp.where(ahead == at, row, 0.0), axis=1, keepdims=True)

    def attend_new():
        padded = -(-steps // 16) * 16
        new_step = lax.broadcasted_iota(jnp.int32, (rows, padded), 1)
        row_index = lax.broadcasted_iota(jnp.int32, (rows, padded), 0)
        allowed = row_index < 0
        for s in range(steps):
            allowed = allowed | ((new_step == s) & (row_index >= s * group))
        for r in range(reqs):
            asked = [query_v[s, r].astype(F32) for s in range(steps)]
            added = [fresh_v[s, r].astype(F32) for s in range(steps)]
            for h in range(heads):
                i = r * heads + h
                query = jnp.concatenate(
                    [a[h * group : (h + 1) * group] for a in asked], axis=0
                ).astype(BF16)
                query_s[i] = query
                latest = jnp.concatenate(
                    [a[h : h + 1] for a in added] + [jnp.zeros((padded - steps, width), F32)],
                    axis=0,
                ).astype(BF16)
                highest, total, weighted = softmax_block(
                    query, latest[:, :depth], latest[:, depth:], allowed, scale
                )
                fresh_o[i] = weighted
                fresh_ml[i, 0:1, :] = to_row((highest, spot[i]))
                fresh_ml[i, 1:2, :] = to_row((total, spot[i]))

    for copy in small[3:]:
        copy.wait()

    @pl.when(core != 0)
    def _():
        attend_new()

    for copy in small[:3]:
        copy.wait()
    aimed = jnp.concatenate([target_v[r] for r in range(reqs)], axis=0)
    weights = jnp.concatenate([weight_v[r].astype(F32) for r in range(reqs)], axis=0)
    owned, position, base = [], jnp.zeros_like(aimed), jnp.zeros(aimed.shape, F32)
    for d in range(shards):
        low = peer(d) * kept
        mine = (aimed >= low) & (aimed < low + kept)
        owned.append(jnp.where(mine, 1.0, 0.0))
        position = jnp.where(mine, aimed - low, position)
        base = jnp.where(mine, float(d * cap), base)
    above = lax.broadcasted_iota(jnp.int32, (evict, evict), 0) < lax.broadcasted_iota(
        jnp.int32, (evict, evict), 1
    )
    earlier = jnp.dot(
        jnp.concatenate(owned, axis=0).astype(BF16),
        jnp.where(above, 1.0, 0.0).astype(BF16),
        preferred_element_type=F32,
    )
    slot = base
    for d in range(shards):
        slot = slot + owned[d] * earlier[d * pairs : (d + 1) * pairs]
    slot = slot.astype(jnp.int32)
    features = jnp.concatenate(
        [weights, (position & 255).astype(F32), (position >> 8).astype(F32)], axis=0
    ).astype(BF16)
    slot_row = lax.broadcasted_iota(jnp.int32, (slots, evict), 0)

    def pack(i):
        r, h = divmod(i, heads)
        packing = jnp.where(slot_row == slot[i : i + 1, :], 1.0, 0.0).astype(BF16)
        packed = jnp.dot(packing, evict_v[r, h], preferred_element_type=F32).astype(BF16)
        send[i] = packed
        recv[i, 0:cap, :] = packed[0:cap]
        meta = contract_last(features, packing)
        meta_send[i : i + 1, :] = (
            (meta[2 * pairs + i : 2 * pairs + i + 1] * 256.0 + meta[pairs + i : pairs + i + 1])
            * 2048.0 + meta[i : i + 1] * 512.0
        )

    others = pl.ds(1, shards - 1)

    def all_of(ref, ssem, rsem):
        return remote(ref, ref, ssem, rsem, peer(1))

    def send_rows(c, d):
        first, count = chunks[c]
        lot = (pl.ds(first, count), pl.ds(d * cap, cap))
        remote(send.at[lot], recv.at[lot], row_ssem.at[0], row_rsem.at[c], peer(d)).start()

    def send_meta(d):
        remote(meta_send, meta_recv.at[d], meta_sem.at[0], meta_sem.at[1], peer(d)).start()

    def rows_in(c):
        first, count = chunks[c]
        lot = (pl.ds(first, count), pl.ds(cap, slots - cap))
        return all_of(recv.at[lot], row_ssem.at[0], row_rsem.at[c])

    def send_rest(m, low, high):
        there = sorted((t for t in range(shards) if t != m), key=lambda t: -abs(t - m))
        edge = m in (0, shards - 1)
        for c in range(low, high):
            for t in there[:-1] if edge else there:
                send_rows(c, (t - m) % shards)
        if edge:
            for c in range(low, high):
                send_rows(c, (there[-1] - m) % shards)

    for i in range(chunks[0][1]):
        pack(i)

    if chain:
        for m in range(shards):
            @pl.when(me == m)
            def _():
                pl.semaphore_wait(barrier, m + (m < shards - 1))
                if 0 < m < shards - 1:
                    tell(near_sem.at[0], m - 1)
                for t in range(m):
                    send_rows(0, (t - m) % shards)
                if m < shards - 1:
                    send_rows(0, 1)

    for i in range(chunks[0][1], pairs):
        pack(i)

    if chain:
        @pl.when(core == 0)
        def _():
            attend_new()

        for m in range(shards):
            @pl.when(me == m)
            def _():
                for far in range(2, shards - m):
                    pl.semaphore_wait(near_sem.at[far - 2], 1)
                    if m > 0:
                        tell(near_sem.at[far - 1], m - 1)
                    send_rows(0, far)
                there = sorted((t for t in range(shards) if t != m), key=lambda t: -abs(t - m))
                for t in there:
                    send_meta((t - m) % shards)

                keep = 0 if 0 < m < shards - 1 else 1

                @pl.when(core == 0)
                def _():
                    send_rest(m, 1, len(chunks) - keep)
    else:
        pl.semaphore_wait(barrier, shards - 1)
        for d in range(1, shards):
            send_meta(d)
        for c in range(len(chunks)):
            for d in range(1, shards):
                send_rows(c, d)

        @pl.when(core == 0)
        def _():
            attend_new()

    meta_in = all_of(meta_recv.at[others], meta_sem.at[0], meta_sem.at[1])
    meta_in.wait_recv()
    lane = lax.broadcasted_iota(jnp.int32, (pairs, slots), 1)
    meta = meta_send[...]
    for d in range(1, shards):
        meta = jnp.where(lane >= d * cap, meta_recv[d], meta)
    slot_position = (meta * (1.0 / 2048.0)).astype(jnp.int32)
    slot_weight = (meta - slot_position.astype(F32) * 2048.0) * (1.0 / 512.0)

    kept_row = lax.broadcasted_iota(jnp.int32, (kept, slots), 0).astype(jnp.int16)
    kept_lane = lax.broadcasted_iota(jnp.int32, (rows, kept), 1)
    ones = jnp.ones((slots, 128), BF16)

    def merge(i):
        r, h = divmod(i, heads)
        aims = jnp.broadcast_to(slot_position[i : i + 1], (16, slots)).astype(jnp.int16)
        gains = jnp.broadcast_to(slot_weight[i : i + 1], (16, slots)).astype(BF16)
        placing = jnp.where(
            kept_row == jnp.concatenate([aims] * (kept // 16), axis=0),
            jnp.concatenate([gains] * (kept // 16), axis=0),
            jnp.zeros((kept, slots), BF16),
        )
        factor = 1.0 / (1.0 + jnp.dot(placing, ones, preferred_element_type=F32))
        if i == 0:
            load.wait()
        for c, (first, _) in enumerate(chunks):
            if first == i:
                rows_in(c).wait_recv()
        if chain and i == 0:
            for m in range(shards):
                @pl.when((me == m) & (core != 0))
                def _():
                    send_rest(m, 1, len(chunks))

                keep = 0 if 0 < m < shards - 1 else 1
                if keep:
                    @pl.when((me == m) & (core == 0))
                    def _():
                        send_rest(m, len(chunks) - keep, len(chunks))
        summed = jnp.dot(placing, recv[i], preferred_element_type=F32)
        factor = jnp.concatenate([factor] * (width // 128), axis=1)
        fused = ((merged[r, h].astype(F32) + summed) * factor).astype(BF16)
        merged[r, h] = fused
        return softmax_block(
            query_s[i], fused[:, :depth], fused[:, depth:], kept_lane < counts_v[:, r : r + 1], scale
        )

    def to_owner(k, count, owner):
        lot = pl.ds(0, count * rows)
        away = lax.rem(owner - me + shards, shards)
        return (
            remote(
                part.at[k, lot], part_recv.at[0, away, lot],
                part_ssem.at[k, 0], part_rsem.at[0, 0], owner,
            ),
            remote(
                part_m.at[k], part_m_recv.at[0, away],
                part_ssem.at[k, 1], part_rsem.at[0, 1], owner,
            ),
        )

    def parts_in(k, count):
        lot = pl.ds(0, count * rows)
        return (
            all_of(part_recv.at[0, others, lot], part_ssem.at[k, 0], part_rsem.at[0, 0]),
            all_of(part_m_recv.at[0, others], part_ssem.at[k, 1], part_rsem.at[0, 1]),
        )

    def share_rows(k, j, d):
        lot = shared.at[k, me, pl.ds(j * rows, rows)]
        return remote(lot, lot, share_ssem.at[0], share_rsem.at[k, 0], peer(d))

    def share_tops(k, d):
        lot = shared_m.at[k, me]
        return remote(lot, lot, share_ssem.at[1], share_rsem.at[k, 1], peer(d))

    def shares(k, count):
        lot = pl.ds(0, count * rows)
        return (
            all_of(shared.at[k, others, lot], share_ssem.at[0], share_rsem.at[k, 0]),
            all_of(shared_m.at[k, others], share_ssem.at[1], share_rsem.at[k, 1]),
        )

    def send_result(k, first, count, d):
        lot = result.at[pl.ds(first, count)]
        return remote(lot, lot, res_ssem.at[0], res_rsem.at[k], peer(d))

    owned_plan = [(k, *entry) for k, entry in enumerate(plan) if entry[2] is not None]
    owned_index = {entry[0]: n for n, entry in enumerate(owned_plan)}
    shared_plan = [(k, *entry) for k, entry in enumerate(plan) if entry[2] is None]
    shared_index = {entry[0]: n for n, entry in enumerate(shared_plan)}

    for k, (first, count, owner) in enumerate(plan):
        tops, sums = [], []
        for j in range(count):
            highest, total, weighted = merge(first + j)
            size = jnp.maximum(jnp.max(jnp.abs(weighted), axis=-1, keepdims=True), 1e-30)
            coded = jnp.round(weighted * (32767.0 / size)).astype(jnp.int32).astype(jnp.int16)
            if owner is None:
                into, into_m = shared.at[shared_index[k], me], shared_m.at[shared_index[k], me]
            else:
                into, into_m = part.at[owned_index[k]], part_m.at[owned_index[k]]
            into[j * rows : (j + 1) * rows, :] = coded
            if owner is None:
                for d in range(1, shards):
                    share_rows(shared_index[k], j, d).start()
            at = j * rows
            tops.append(to_row((highest, at), (size * (1.0 / 32767.0), at + 64)))
            sums.append(to_row((total, at)))
        into_m[0:1, :] = functools.reduce(jnp.add, tops)
        into_m[1:2, :] = functools.reduce(jnp.add, sums)
        if owner is None:
            for d in range(1, shards):
                share_tops(shared_index[k], d).start()
        else:
            @pl.when(me != owner)
            def _():
                for copy in to_owner(owned_index[k], count, owner):
                    copy.start()

    lanes = lax.broadcasted_iota(jnp.int32, (1, 128), 1)

    def combine(first, count, blocks):
        group = range(first, first + count)
        tiles = [
            (
                functools.reduce(jnp.add, [fresh_ml[i, 0:1, :] for i in group]),
                functools.reduce(jnp.add, [fresh_ml[i, 1:2, :] for i in group]),
            )
        ] + [(m[0:1, :], m[1:2, :]) for _, m in blocks]
        top = functools.reduce(jnp.maximum, [tile[0] for tile in tiles])
        shares = [jnp.exp(tile[0] - top) for tile in tiles]
        total = functools.reduce(jnp.add, [a * tile[1] for a, tile in zip(shares, tiles)])
        shares = [a / jnp.where(lanes < count * rows, total, 1.0) for a in shares]
        for n, (_, m) in enumerate(blocks):
            scales = jnp.concatenate([m[0:1, 64:], m[0:1, :64]], axis=1)
            shares[n + 1] = shares[n + 1] * scales
        for j, i in enumerate(group):
            blend = to_column(shares[0], j * rows) * fresh_o[i]
            for share, (b, _) in zip(shares[1:], blocks):
                out = b[j * rows : (j + 1) * rows, :].astype(jnp.int32).astype(F32)
                blend = blend + to_column(share, j * rows) * out
            result[i] = blend.astype(BF16)

    for k, first, count, owner in owned_plan:
        n = owned_index[k]

        @pl.when(me == owner)
        def _():
            for copy in parts_in(n, count):
                copy.wait_recv()
            combine(
                first, count,
                [(part.at[n], part_m.at[n])]
                + [(part_recv.at[0, d], part_m_recv.at[0, d]) for d in range(1, shards)],
            )
            for d in range(1, shards):
                send_result(n, first, count, d).start()

    for k, first, count, _ in shared_plan:
        n = shared_index[k]
        for copy in shares(n, count):
            copy.wait_recv()
        combine(first, count, [(shared.at[n, d], shared_m.at[n, d]) for d in range(shards)])

    for k, first, count, owner in owned_plan:
        @pl.when(me != owner)
        def _():
            send_result(owned_index[k], first, count, 1).wait_recv()

    for r in range(reqs):
        done = [result[r * heads + h].astype(F32) for h in range(heads)]
        for s in range(steps):
            attended[s, r] = jnp.concatenate(
                [a[s * group : (s + 1) * group] for a in done], axis=0
            ).astype(BF16)

    meta_in.wait_send()
    sent = (pl.ds(0, pairs), pl.ds(cap, slots - cap))
    all_of(recv.at[sent], row_ssem.at[0], row_rsem.at[0]).wait_send()
    for k, first, count, owner in owned_plan:
        n = owned_index[k]

        @pl.when(me != owner)
        def _():
            for copy in to_owner(n, count, owner):
                copy.wait_send()

        @pl.when(me == owner)
        def _():
            lot = part_recv.at[0, others, pl.ds(0, count * rows)]
            all_of(lot, res_ssem.at[0], res_rsem.at[n]).wait_send()

    if shared_plan:
        gone = (pl.ds(0, len(shared_plan)), others)
        lot = (*gone, pl.ds(0, shared_plan[0][2] * rows))
        all_of(shared.at[lot], share_ssem.at[0], share_rsem.at[0, 0]).wait_send()
        all_of(shared_m.at[gone], share_ssem.at[1], share_rsem.at[0, 1]).wait_send()


def write_out(merged, attended, merged_out, attended_out, sem):
    copies = [
        pltpu.make_async_copy(merged, merged_out, sem.at[0]),
        pltpu.make_async_copy(attended, attended_out, sem.at[1]),
    ]
    for copy in copies:
        copy.start()
    for copy in copies:
        copy.wait()


def schedule(shards, pairs):
    per = max(1, min(2, pairs // shards))
    firsts = list(range(0, pairs, per))
    near = shards <= 8
    late = len(firsts) // 2 if near else 0
    plan = []
    for n, first in enumerate(firsts):
        owner = (shards // 2 - 1 + n) % shards if near else n % shards
        plan.append((first, min(per, pairs - first), owner if n < len(firsts) - late else None))
    return tuple(plan)


def row_chunks(shards, pairs):
    if shards > 8 or shards < 3:
        return ((0, pairs),)
    head = max(1, 3 * pairs // 8)
    return ((0, head),) + tuple((i, 1) for i in range(head, pairs))


def body(shards, cache, evicted, merge_weight, targets, kept_counts, queries, new_rows):
    reqs, heads, kept, width = cache.shape
    pairs = reqs * heads
    evict = evicted.shape[2]
    steps, _, query_local, depth = queries.shape
    rows = steps * query_local // heads
    cap = -(-max(2, 2 * evict // shards) // 16) * 16
    slots = shards * cap
    chunks = row_chunks(shards, pairs)
    plan = schedule(shards, pairs)
    most = max(count for _, count, _ in plan)
    owned = max(1, sum(owner is not None for _, _, owner in plan))
    common = max(1, len(plan) - owned)
    assert most * rows <= 64
    high = 2
    dma = pltpu.SemaphoreType.DMA
    done = pl.pallas_call(
        functools.partial(kernel, shards, cap, chunks, plan),
        out_shape=(
            jax.ShapeDtypeStruct(cache.shape, BF16),
            jax.ShapeDtypeStruct(queries.shape, BF16),
        ),
        in_specs=[pl.BlockSpec(memory_space=pltpu.HBM)] * 7,
        out_specs=(pl.BlockSpec(memory_space=pltpu.VMEM),) * 2,
        scratch_shapes=[
            pltpu.VMEM(evicted.shape, BF16),
            pltpu.VMEM(merge_weight.shape, BF16),
            pltpu.VMEM(targets.shape, jnp.int32),
            pltpu.VMEM(kept_counts.shape[::-1], jnp.int32),
            pltpu.VMEM(queries.shape, BF16),
            pltpu.VMEM(new_rows.shape, BF16),
            pltpu.VMEM((pairs, slots, width), BF16),
            pltpu.VMEM((pairs, slots, width), BF16),
            pltpu.VMEM((pairs, slots), F32),
            pltpu.VMEM((shards, pairs, slots), F32),
            pltpu.VMEM((pairs, rows, depth), BF16),
            pltpu.VMEM((pairs, rows, depth), F32),
            pltpu.VMEM((pairs, 2, 128), F32),
            pltpu.VMEM((owned, most * rows, depth), jnp.int16),
            pltpu.VMEM((owned, high, 128), F32),
            pltpu.VMEM((1, shards, most * rows, depth), jnp.int16),
            pltpu.VMEM((1, shards, high, 128), F32),
            pltpu.VMEM((common, shards, most * rows, depth), jnp.int16),
            pltpu.VMEM((common, shards, high, 128), F32),
            pltpu.VMEM((pairs, rows, depth), BF16),
            pltpu.SemaphoreType.REGULAR((max(1, shards - 2),)),
            dma((6,)),
            dma((1,)),
            dma((1,)),
            dma((len(chunks),)),
            dma((2,)),
            dma((owned, 2)),
            dma((1, 2)),
            dma((2,)),
            dma((common, 2)),
            dma((1,)),
            dma((owned,)),
        ],
        compiler_params=pltpu.CompilerParams(
            collective_id=0, has_side_effects=True, vmem_limit_bytes=48 * 1024 * 1024
        ),
    )(*(
        pltpu.with_memory_space_constraint(a, pltpu.HBM)
        for a in (cache, evicted, merge_weight, targets, kept_counts.T, queries, new_rows)
    ))
    return pl.pallas_call(
        write_out,
        out_shape=tuple(jax.ShapeDtypeStruct(a.shape, a.dtype) for a in done),
        in_specs=[pl.BlockSpec(memory_space=pltpu.VMEM)] * 2,
        out_specs=(pl.BlockSpec(memory_space=pltpu.HBM),) * 2,
        scratch_shapes=[dma((2,))],
    )(*(pltpu.with_memory_space_constraint(a, pltpu.VMEM) for a in done))


def solution(mesh):
    return jax.shard_map(
        functools.partial(body, mesh.shape["seq"]),
        mesh=mesh,
        in_specs=(
            P(("grp", "req"), "hd", "seq", None),
            P(("grp", "req"), "hd", "seq", None),
            P(("grp", "req"), "hd", "seq"),
            P(("grp", "req"), "hd", "seq"),
            P(("grp", "req"), "seq"),
            P(None, ("grp", "req"), "hd", None),
            P(None, ("grp", "req"), "hd", None),
        ),
        out_specs=(P(("grp", "req"), "hd", "seq", None), P(None, ("grp", "req"), "hd", None)),
        check_vma=False,
    )
```
